32 devices in a mesh: dp: 16 (over z, x, core), seq: 2 (over y).
Axes of the slice: x: 2, y: 2, z: 4, core: 2. Of those that a mesh axis runs over, the one named last changes fastest.
Arguments:
- queries: bfloat16 [16, 256, 1024], P('dp', 'seq'), may hold values from -6 to 6
- keys: bfloat16 [16, 256, 1024], P('dp', 'seq'), may hold values from -6 to 6
- values: bfloat16 [16, 256, 1024], P('dp', 'seq'), may hold values from -6 to 6
- stream: bfloat16 [16, 256, 1024], P('dp', 'seq'), may hold values from -6 to 6
- cotangent: bfloat16 [16, 256, 1024], P('dp', 'seq'), may hold values from -6 to 6
- attn_out: bfloat16 [1024, 1024], replicated, may hold values from -0.1875 to 0.1875
- point_in: bfloat16 [1024, 2048], replicated, may hold values from -0.1875 to 0.1875
- kernel: bfloat16 [31, 1024], replicated, may hold values from -1 to 1
- point_out: bfloat16 [1024, 1024], replicated, may hold values from -0.1875 to 0.1875
- norm_gain: float32 [1024], replicated, may hold values from 0.1 to 1.9
- conv_gain: float32 [1024], replicated, may hold values from 0.1 to 1.9
- segments: int32 [16, 256], replicated, may hold values from 0 to 127, as said below
- plan: int32 [16], replicated, may hold values from 0 to 15, as said below
Outputs:
- query_grad: bfloat16 [16, 256, 1024], P('dp', 'seq')
- key_grad: bfloat16 [16, 256, 1024], P('dp', 'seq')
- value_grad: bfloat16 [16, 256, 1024], P('dp', 'seq')
- stream_grad: bfloat16 [16, 256, 1024], P('dp', 'seq')
- kernel_grad: float32 [31, 1024], replicated
- proj_grads: float32 [1024, 2048], P(('dp', 'seq'))
The draws below stay inside these ranges and needn't reach their ends.
Inputs may be any that keep to these rules, and one draw needn't show every extreme that they name: `segments`: along each pack the numbers never fall and change only at even frames; one number marks one utterance. `plan`: A permutation of 0 to 15.
All inputs are finite; a program needn't handle non-finite values.
Results may differ from the reference program's by a relative error of at most 0.024.
Values may be sent and summed in bfloat16 or wider, within the bound.
A program may use at most 128 MiB of HBM per device.

```python
import jax
import jax.numpy as jnp
from jax import lax

D = 1024
HEADS = 16
KERNEL = 31
HEAD_DIM = 64
LENGTH = 256
PACKS = 16


def draw_queries(key, part):
    fresh = jnp.clip(jax.random.normal(jax.random.fold_in(key, 1), (PACKS, LENGTH, D)), -6.0, 6.0)
    return fresh.astype(jnp.bfloat16)


def draw_keys(key, part):
    fresh = jnp.clip(jax.random.normal(jax.random.fold_in(key, 2), (PACKS, LENGTH, D)), -6.0, 6.0)
    return fresh.astype(jnp.bfloat16)


def draw_segments(key, part):
    level_key, flag_key = jax.random.split(jax.random.fold_in(key, 3))
    level = jax.random.randint(level_key, (PACKS, 1), 0, 4)
    limits = jnp.array([0, 2048, 16384, 131072], jnp.int32)
    thresh = jnp.sum(jnp.where(level == jnp.arange(4)[None, :], limits[None, :], 0), 1, keepdims=True)
    draws = jax.random.randint(flag_key, (PACKS, LENGTH // 2), 0, 1048576)
    flags = (draws < thresh).astype(jnp.int32) * (jnp.arange(LENGTH // 2) > 0).astype(jnp.int32)[None, :]
    pairs = jnp.cumsum(flags, 1).astype(jnp.int32)
    odd = (jnp.arange(PACKS) % 2).astype(jnp.int32)[:, None]
    lift = (LENGTH // 2 - 1 - pairs[:, -1:]) * odd
    return jnp.repeat(pairs + lift, 2, axis=1).astype(jnp.int32)


def draw_plan(key, part):
    return jax.random.permutation(jax.random.fold_in(key, 5), PACKS).astype(jnp.int32)


def shard_levels(stream_key, extent, cuts, smallest, largest):
    factor_of, own = 1.0, jax.random.fold_in(stream_key, 6)
    for axis_at, parts in cuts:
        heights = jnp.exp(jax.random.uniform(jax.random.fold_in(own, axis_at), (parts,), jnp.float32, smallest / len(cuts), largest / len(cuts)))
        factor_of = factor_of * jnp.repeat(heights, extent[axis_at] // parts).reshape([-1 if axis == axis_at else 1 for axis in range(len(extent))])
    return factor_of


def centred(key, dims, deviation, bound, shards=(), held_as=jnp.bfloat16):
    values = deviation * jax.random.normal(key, dims, jnp.float32)
    if shards:
        values = values * shard_levels(key, dims, shards, -0.22, 0.18)
    return jnp.clip(values, -bound, bound).astype(held_as)


def setup_inputs(seed: int = 0) -> dict:
    splits = jax.random.split(jax.random.key(seed), 14)
    queries = draw_queries(jax.random.fold_in(splits[13], 71), 0)
    keys = draw_keys(jax.random.fold_in(splits[13], 71), 0)
    values = centred(splits[2], (PACKS, LENGTH, D), 1.0, 6.0, ((0, 16), (1, 2)))
    stream = centred(splits[3], (PACKS, LENGTH, D), 1.0, 6.0, ((0, 16), (1, 2)))
    cotangent = centred(splits[4], (PACKS, LENGTH, D), 1.0, 6.0, ((0, 16), (1, 2)))
    attn_out = centred(splits[5], (D, D), D ** -0.5, 0.1875)
    point_in = centred(splits[6], (D, 2 * D), D ** -0.5, 0.1875)
    kernel = centred(splits[7], (KERNEL, D), KERNEL ** -0.5, 1.0)
    point_out = centred(splits[8], (D, D), D ** -0.5, 0.1875)
    norm_gain = jnp.clip(1.0 + 0.18 * jax.random.normal(splits[9], (D,), jnp.float32), 0.1, 1.9)
    conv_gain = jnp.clip(1.0 + 0.18 * jax.random.normal(splits[10], (D,), jnp.float32), 0.1, 1.9)
    segments = draw_segments(jax.random.fold_in(splits[13], 71), 0)
    plan = draw_plan(jax.random.fold_in(splits[13], 71), 0)
    return {"queries": queries, "keys": keys, "values": values, "stream": stream, "cotangent": cotangent, "attn_out": attn_out, "point_in": point_in, "kernel": kernel, "point_out": point_out, "norm_gain": norm_gain, "conv_gain": conv_gain, "segments": segments, "plan": plan}


EPSILON = 1e-05
MASKED = -1e+30

def layer_norm(stream, gain):
    center = lax.optimization_barrier(jnp.mean(stream, -1, keepdims=True))
    shifted = stream - center
    inverse = lax.rsqrt(lax.optimization_barrier(jnp.mean(shifted * shifted, -1, keepdims=True)) + EPSILON)
    normed = shifted * inverse
    return (normed * gain, normed, inverse)

def norm_backward(upstream, normed, inverse, gain):
    scaled = upstream * gain
    return inverse * (scaled - lax.optimization_barrier(jnp.mean(scaled, -1, keepdims=True)) - normed * lax.optimization_barrier(jnp.mean(scaled * normed, -1, keepdims=True)))

def swish_slope(values):
    logistic = jax.nn.sigmoid(values)
    return logistic * (1.0 + values * (1.0 - logistic))

def tap_table(padded_ids, own_ids, taps):
    length = own_ids.shape[0]
    return (jnp.stack([padded_ids[tap:tap + length] for tap in range(taps)], 1) == own_ids[:, None]).astype(jnp.float32)

def depthwise(padded, weights, table):
    length = table.shape[0]
    total = jnp.zeros((length, padded.shape[1]), jnp.float32)
    for tap in range(weights.shape[0]):
        total = total + weights[tap].astype(jnp.float32) * padded[tap:tap + length].astype(jnp.float32) * table[:, tap:tap + 1]
    return total

def tap_sums(upstream, padded, table):
    length = table.shape[0]
    return jnp.stack([lax.optimization_barrier(jnp.sum(upstream * padded[tap:tap + length].astype(jnp.float32) * table[:, tap:tap + 1], 0)) for tap in range(table.shape[1])])

def split_heads(matrix):
    return matrix.reshape(matrix.shape[0], HEADS, HEAD_DIM).transpose(1, 0, 2)

def merge_heads(tensor):
    return tensor.transpose(1, 0, 2).reshape(tensor.shape[1], -1)

def head_weights(query_head, key_head, ids):
    scores = jnp.dot(query_head, key_head.T, preferred_element_type=jnp.float32) * HEAD_DIM ** (-0.5)
    scores = jnp.where(ids[:, None] == ids[None, :], scores, MASKED)
    highest = lax.optimization_barrier(jnp.max(scores, -1, keepdims=True))
    log_total = highest + jnp.log(lax.optimization_barrier(jnp.sum(jnp.exp(scores - highest), -1, keepdims=True)))
    return jnp.exp(scores - log_total)

def pack_pass(queries, keys, values, stream, cotangent, ids, attn_out, point_in, kernel, point_out, norm_gain, conv_gain):

    def forward_head(items):
        query_head, key_head, value_head = items
        weights = head_weights(query_head, key_head, ids)
        return jnp.dot(weights.astype(jnp.bfloat16), value_head, preferred_element_type=jnp.float32).astype(jnp.bfloat16)
    query_heads, key_heads, value_heads = (split_heads(queries), split_heads(keys), split_heads(values))
    mixed = merge_heads(lax.map(forward_head, (query_heads, key_heads, value_heads)))
    hidden = stream.astype(jnp.float32) + jnp.dot(mixed, attn_out, preferred_element_type=jnp.float32)
    normed_in, hat_in, inv_in = layer_norm(hidden, norm_gain)
    both = jnp.dot(normed_in.astype(jnp.bfloat16), point_in, preferred_element_type=jnp.float32)
    linear = both[:, :D]
    logistic = jax.nn.sigmoid(both[:, D:])
    conv_in = (linear * logistic).astype(jnp.bfloat16)
    reach = KERNEL // 2
    padded = jnp.pad(conv_in, ((reach, reach), (0, 0)))
    table = tap_table(jnp.pad(ids, reach, constant_values=-1), ids, KERNEL)
    conv_out = depthwise(padded, kernel, table)
    normed_out, hat_out, inv_out = layer_norm(conv_out, conv_gain)
    activated = (normed_out * jax.nn.sigmoid(normed_out)).astype(jnp.bfloat16)
    act_grad = jnp.dot(cotangent, point_out.T, preferred_element_type=jnp.float32)
    conv_grad = norm_backward(act_grad * swish_slope(normed_out), hat_out, inv_out, conv_gain)
    kernel_part = tap_sums(conv_grad, padded, table)
    in_grad = depthwise(jnp.pad(conv_grad, ((reach, reach), (0, 0))), kernel[::-1], table)
    both_grad = jnp.concatenate([in_grad * logistic, in_grad * linear * logistic * (1.0 - logistic)], 1).astype(jnp.bfloat16)
    back_in = jnp.dot(both_grad, point_in.T, preferred_element_type=jnp.float32)
    stream_out = (cotangent.astype(jnp.float32) + norm_backward(back_in, hat_in, inv_in, norm_gain)).astype(jnp.bfloat16)
    mixed_grad = jnp.dot(stream_out, attn_out.T, preferred_element_type=jnp.float32).astype(jnp.bfloat16)
    scale = HEAD_DIM ** (-0.5)

    def backward_head(items):
        query_head, key_head, value_head, grad_head = items
        weights = head_weights(query_head, key_head, ids)
        slope = jnp.dot(grad_head, value_head.T, preferred_element_type=jnp.float32)
        delta = lax.optimization_barrier(jnp.sum(weights * slope, -1, keepdims=True))
        score_grad = (weights * (slope - delta)).astype(jnp.bfloat16)
        query_part = (jnp.dot(score_grad, key_head, preferred_element_type=jnp.float32) * scale).astype(jnp.bfloat16)
        key_part = (jnp.dot(score_grad.T, query_head, preferred_element_type=jnp.float32) * scale).astype(jnp.bfloat16)
        value_part = jnp.dot(weights.astype(jnp.bfloat16).T, grad_head, preferred_element_type=jnp.float32).astype(jnp.bfloat16)
        return (query_part, key_part, value_part)
    query_part, key_part, value_part = lax.map(backward_head, (query_heads, key_heads, value_heads, split_heads(mixed_grad)))
    proj_part = jnp.concatenate([jnp.dot(mixed.T, stream_out, preferred_element_type=jnp.float32), jnp.dot(activated.T, cotangent, preferred_element_type=jnp.float32)], 1)
    return (merge_heads(query_part), merge_heads(key_part), merge_heads(value_part), stream_out, kernel_part, proj_part)

def reference(queries, keys, values, stream, cotangent, attn_out, point_in, kernel, point_out, norm_gain, conv_gain, segments, plan):

    def one_slot(carry, slot):
        source = plan[slot]
        results = pack_pass(queries[source], keys[source], values[source], stream[source], cotangent[source], segments[source], attn_out, point_in, kernel, point_out, norm_gain, conv_gain)
        return ((carry[0] + results[4], carry[1] + results[5]), (results[0], results[1], results[2], results[3]))
    start = (jnp.zeros((KERNEL, D), jnp.float32), jnp.zeros((D, 2 * D), jnp.float32))
    totals, slots = lax.scan(one_slot, start, jnp.arange(PACKS))
    return (slots[0], slots[1], slots[2], slots[3], totals[0], totals[1])
```

```python
import functools
import types

import jax
import jax.numpy as jnp
from jax import lax
from jax.experimental import pallas as pl
from jax.experimental.pallas import tpu as pltpu
from jax.sharding import PartitionSpec as P

HEAD_DIM = 64
EPSILON = 1e-05
MASKED = -1e30
LANES = 128
TILE = 256
SUB = 16
F32 = jnp.float32
BF16 = jnp.bfloat16


def dot(left, right):
    return jnp.dot(left, right, preferred_element_type=F32)


def dot_t(left, right):
    return lax.dot_general(left, right, (((1,), (1,)), ((), ())), preferred_element_type=F32)


def t_dot(left, right):
    return lax.dot_general(left, right, (((0,), (0,)), ((), ())), preferred_element_type=F32)


def loop(count, body):
    def step(i, carry):
        body(i)
        return carry

    lax.fori_loop(0, count, step, 0)


def span(i, size):
    return pl.ds(pl.multiple_of(i * size, size), size)


def log2(count):
    return (count - 1).bit_length()


def chunking(count, rows, width):
    down = min(count, rows // SUB)
    across = count // down
    return rows // down, width // across, across


def bits_of(n, q):
    seqs = log2(q)
    return (
        [("dp", bit, seqs + bit) for bit in range(min(1, log2(n)))]
        + [("seq", bit, bit) for bit in range(seqs)]
        + [("dp", bit, seqs + bit) for bit in range(1, log2(n))]
    )


def split_bits(n, q, width):
    low = 0
    while (width >> (log2(n) + log2(q) - low)) < SUB:
        low += 1
    order = bits_of(n, q)
    return [e for e in order if e[2] >= low], [e for e in order if e[2] < low], low


def runs_of(blocks, rows):
    runs = []
    for block in blocks:
        if runs and runs[-1][0] + runs[-1][1] == block * rows:
            runs[-1][1] += rows
        else:
            runs.append([block * rows, rows])
    return runs


def schedule(order, sequence, rows):
    depth = len(order)
    kept = list(range(1 << depth))
    plan = []
    for which in sequence:
        bit = 1 << (depth - 1 - which)
        plan.append((order[which], runs_of([u for u in kept if u & bit], rows), runs_of([u for u in kept if not u & bit], rows)))
        kept = [u for u in kept if not u & bit]
    return plan


def body(n, q, names, *refs):
    r = types.SimpleNamespace(**dict(zip(names, refs)))
    frames, width = r.x_in.shape
    whole = q * frames
    taps = r.kernel.shape[0]
    reach = taps // 2
    pairs = width // LANES
    parts = width // TILE
    tiles = width // TILE
    rows_c, cols_c, across = chunking(n, frames, width)
    me_d, me_s = lax.axis_index("dp"), lax.axis_index("seq")
    scale = HEAD_DIM ** (-0.5)
    order, _, low = split_bits(n, q, width)

    def remote(src, dst, ssem, rsem, dp=None, seq=None):
        return pltpu.make_async_remote_copy(
            src_ref=src,
            dst_ref=dst,
            send_sem=ssem,
            recv_sem=rsem,
            device_id=(me_d if dp is None else dp, me_s if seq is None else seq),
            device_id_type=pl.DeviceIdType.MESH,
        )

    def drain(view, sem):
        pltpu.make_async_copy(view, view, sem).wait()

    def flipped(place, bit):
        mine = lax.rem(place // (1 << bit), 2)
        return place + (1 - 2 * mine) * (1 << bit)

    def partner(entry):
        axis, bit, _ = entry
        if axis == "dp":
            return dict(dp=flipped(me_d, bit))
        return dict(seq=flipped(me_s, bit))

    loads = [
        (r.keys.at[0], r.k_all.at[pl.ds(0, frames)]),
        (r.values.at[0], r.v_all.at[pl.ds(0, frames)]),
        (r.cotangent.at[0], r.g_in),
        (r.point_out, r.po),
        (r.queries.at[0], r.q_in),
        (r.stream.at[0], r.x_in),
        (r.attn_out, r.ao),
        (r.point_in, r.pin),
    ]
    loads = [pltpu.make_async_copy(src, dst, r.load_sem.at[at]) for at, (src, dst) in enumerate(loads)]
    for copy in loads:
        copy.start()
    load_k, load_v, load_g, load_po, load_q, load_x, load_ao, load_pin = loads

    barrier = pltpu.get_barrier_semaphore()

    def greet_dp(step):
        pl.semaphore_signal(
            barrier, inc=1, device_id=(lax.rem(me_d + 1 + step, n), me_s), device_id_type=pl.DeviceIdType.MESH
        )

    def greet_seq(step):
        pl.semaphore_signal(
            barrier, inc=1, device_id=(me_d, lax.rem(me_s + 1 + step, q)), device_id_type=pl.DeviceIdType.MESH
        )

    loop(n - 1, greet_dp)
    loop(q - 1, greet_seq)
    pl.semaphore_wait(barrier, n + q - 2)

    def pair_copy(which, step, part):
        source, target = ((r.keys, r.k_all), (r.values, r.v_all))[which]
        at = ((step - 1) * parts + part) * 2 + which
        return remote(
            source.at[0, :, span(part, TILE)],
            target.at[pl.ds(step * frames, frames), span(part, TILE)],
            r.kv_send.at[at],
            r.kv_recv.at[at],
            seq=lax.rem(me_s + q - step, q),
        )

    def send_part(part):
        for step in range(1, q):
            for which in range(2):
                pair_copy(which, step, part).start()

    loop(parts, send_part)

    def piece(place):
        return (
            pl.ds(pl.multiple_of((place // across) * rows_c, rows_c), rows_c),
            pl.ds(pl.multiple_of(lax.rem(place, across) * cols_c, cols_c), cols_c),
        )

    def spread(sources, inter, ssem, rsem):
        def send(step):
            to = lax.rem(me_d + 1 + step, n)
            at = piece(to)
            for a, source in enumerate(sources):
                remote(source.at[at[0], at[1]], inter.at[a, me_d], ssem, rsem, dp=to).start()

        loop(n - 1, send)

    def spread_own(sources, inter):
        at = piece(me_d)
        for a, source in enumerate(sources):
            inter[a, me_d] = source[at[0], at[1]]

    def spread_done(count, inter, ssem, rsem):
        view = inter.at[:, pl.ds(0, n - 1)]
        drain(view, rsem)
        drain(view, ssem)

    def deliver(count, inter, stage, target, ssem, rsem):
        at = piece(me_d)

        def send(step):
            to = lax.rem(me_d + 1 + step, n)
            for a in range(count):
                stage[a, to] = inter[a, r.plan[to]]
                remote(stage.at[a, to], target.at[a, at[0], at[1]], ssem, rsem, dp=to).start()

        loop(n - 1, send)
        for a in range(count):
            target[a, at[0], at[1]] = inter[a, r.plan[me_d]]

    def deliver_done(count, stage, ssem, rsem):
        view = stage.at[:, pl.ds(0, n - 1)]
        drain(view, rsem)
        drain(view, ssem)

    def widen(target, count, ssem, rsem):
        out = []
        for step in range(1, q):
            for a in range(count):
                at = (step - 1) * count + a
                out.append(
                    remote(
                        target.at[a, pl.ds(0, frames)],
                        target.at[a, pl.ds(step * frames, frames)],
                        ssem.at[at],
                        rsem.at[at],
                        seq=lax.rem(me_s + q - step, q),
                    )
                )
        return out

    spread(
        [r.queries.at[0], r.keys.at[0], r.values.at[0]], r.inter, r.route_sem.at[0], r.route_sem.at[1]
    )

    def row_ids(row, step):
        block = lax.rem(me_s + step + q, q)
        line = r.segments[pl.ds(row, 1), :]
        chosen = line[:, :frames]
        for b in range(1, q):
            chosen = jnp.where(block == b, line[:, b * frames : (b + 1) * frames], chosen)
        return chosen.astype(F32)

    def col_ids(row, step):
        return jnp.broadcast_to(row_ids(row, step), (LANES, frames)).T

    own_col = col_ids(me_d, 0)
    for step in range(q):
        r.bias[:, pl.ds(step * frames, frames)] = jnp.where(own_col[:, :1] == row_ids(me_d, step), 0.0, MASKED)
    before = jnp.where(me_s > 0, col_ids(me_d, -1)[frames - SUB :], -1.0)
    after = jnp.where(me_s < q - 1, col_ids(me_d, 1)[:SUB], -1.0)
    r.id_pad[pl.ds(0, SUB)] = before
    r.id_pad[pl.ds(SUB, frames)] = own_col
    r.id_pad[pl.ds(SUB + frames, SUB)] = after
    for tap in range(taps):
        r.same[tap] = jnp.where(r.id_pad[pl.ds(SUB - reach + tap, frames)] == own_col, 1.0, 0.0)
    r.taps_f[pl.ds(0, taps)] = r.kernel[...].astype(F32)
    slot_pack = r.plan[me_d]
    for b in range(q):
        col = col_ids(slot_pack, b)
        for step in range(q):
            r.slot_bias[pl.ds(b * frames, frames), pl.ds(step * frames, frames)] = jnp.where(
                col[:, :1] == row_ids(slot_pack, step), 0.0, MASKED
            )

    load_g.wait()
    load_po.wait()

    def act_tile(i):
        r.act_grad[:, span(i, TILE)] = dot_t(r.g_in[...], r.po[span(i, TILE), :])

    loop(tiles, act_tile)

    lane = lax.broadcasted_iota(jnp.int32, (1, LANES), 1)
    first = jnp.where(lane < HEAD_DIM, 1.0, 0.0)
    heads_low = (first.astype(BF16), (1.0 - first).astype(BF16))

    def stacked(two, factor=1.0):
        return jnp.concatenate([two * (h * factor).astype(BF16) for h in heads_low], 0)

    def merged(tall):
        return jnp.where(lane < HEAD_DIM, tall[:frames], tall[frames:])

    def softmax(scores, bias):
        scores = scores + jnp.concatenate([bias, bias], 0)
        raised = jnp.exp(scores - jnp.max(scores, -1, keepdims=True))
        return raised * (1.0 / jnp.sum(raised, -1, keepdims=True))

    load_q.wait()
    load_k.wait()
    load_v.wait()
    spread_own([r.q_in, r.k_all, r.v_all], r.inter)

    def attend_part(part):
        for step in range(1, q):
            for which in range(2):
                pair_copy(which, step, part).wait()

        def attend(i):
            at = span(part * (TILE // LANES) + i, LANES)
            weights = softmax(dot_t(stacked(r.q_in[:, at], scale), r.k_all[:, at]), r.bias[...])
            r.mixed[:, at] = merged(dot(weights.astype(BF16), r.v_all[:, at])).astype(BF16)

        loop(TILE // LANES, attend)

    loop(parts, attend_part)

    load_x.wait()
    load_ao.wait()

    def hidden_tile(i):
        at = span(i, TILE)
        r.hat_in[:, at] = r.x_in[:, at].astype(F32) + dot(r.mixed[...], r.ao[:, at])

    loop(tiles, hidden_tile)

    def norm_rows(i):
        at = span(i, SUB)
        hidden = r.hat_in[at, :]
        shifted = hidden - jnp.mean(hidden, -1, keepdims=True)
        inverse = lax.rsqrt(jnp.mean(shifted * shifted, -1, keepdims=True) + EPSILON)
        normed = shifted * inverse
        r.hat_in[at, :] = normed
        r.inv_in[at, :] = jnp.broadcast_to(inverse, (SUB, LANES))
        r.low[at, :] = (normed * r.norm_gain[...]).astype(BF16)

    loop(frames // SUB, norm_rows)
    load_pin.wait()

    def gate_tile(i):
        at = span(i, TILE)
        linear = dot(r.low[...], r.pin[:, at])
        logistic = jax.nn.sigmoid(dot(r.low[...], r.pin[:, span(i + tiles, TILE)]))
        conv_in = (linear * logistic).astype(BF16)
        r.linear[:, at] = linear
        r.logistic[:, at] = logistic
        r.conv_in[:, at] = conv_in
        wide = conv_in.astype(F32)
        for c in range(TILE // LANES):
            r.x_pad[i * (TILE // LANES) + c, pl.ds(SUB, frames), :] = wide[:, c * LANES : (c + 1) * LANES]

    loop(tiles, gate_tile)

    def edges(source, halo, at):
        return (
            remote(
                source.at[pl.ds(frames - SUB, SUB)],
                halo.at[0],
                r.edge_send.at[at],
                r.edge_recv.at[at],
                seq=lax.rem(me_s + 1, q),
            ),
            remote(
                source.at[pl.ds(0, SUB)],
                halo.at[1],
                r.edge_send.at[at + 1],
                r.edge_recv.at[at + 1],
                seq=lax.rem(me_s + q - 1, q),
            ),
        )

    def land(halo, pad):
        def put(c):
            at = span(c, LANES)
            pad[c, pl.ds(0, SUB), :] = halo[0, :, at].astype(F32)
            pad[c, pl.ds(SUB + frames, SUB), :] = halo[1, :, at].astype(F32)

        loop(pairs, put)

    edge_in = edges(r.conv_in, r.halo_in, 0)
    for copy in edge_in:
        copy.start()

    spread_done(3, r.inter, r.route_sem.at[0], r.route_sem.at[1])
    deliver(3, r.inter, r.stage, r.slot, r.route_sem.at[2], r.route_sem.at[3])

    for copy in edge_in:
        copy.wait()
    land(r.halo_in, r.x_pad)

    def conv_tile(c):
        total = jnp.zeros((frames, LANES), F32)
        for tap in range(taps):
            moved = r.x_pad[c, pl.ds(SUB - reach + tap, frames), :] * r.same[tap]
            total = total + r.taps_f[tap : tap + 1, span(c, LANES)] * moved
        r.work[:, span(c, LANES)] = total

    loop(pairs, conv_tile)

    def mid_rows(i):
        at = span(i, SUB)
        conv = r.work[at, :]
        shifted = conv - jnp.mean(conv, -1, keepdims=True)
        inverse = lax.rsqrt(jnp.mean(shifted * shifted, -1, keepdims=True) + EPSILON)
        hat = shifted * inverse
        gain = r.conv_gain[...]
        normed = hat * gain
        logistic = jax.nn.sigmoid(normed)
        r.low[at, :] = (normed * logistic).astype(BF16)
        scaled = r.act_grad[at, :] * (logistic * (1.0 + normed * (1.0 - logistic))) * gain
        grad = inverse * (
            scaled - jnp.mean(scaled, -1, keepdims=True) - hat * jnp.mean(scaled * hat, -1, keepdims=True)
        )
        r.conv_grad[at, :] = grad.astype(BF16)
        for c in range(pairs):
            r.g_pad[c, pl.ds(pl.multiple_of(i * SUB + SUB, SUB), SUB), :] = grad[:, c * LANES : (c + 1) * LANES]

    loop(frames // SUB, mid_rows)
    edge_out = edges(r.conv_grad, r.halo_out, 2)
    for copy in edge_out:
        copy.start()

    depth = len(order)
    gran = width >> depth
    swap = list(range(depth))
    seqs = len([e for e in order if e[0] == "seq"])
    if depth > 1 + seqs and seqs:
        swap = [0, 1 + seqs] + list(range(1, 1 + seqs)) + list(range(2 + seqs, depth))
    half_cols = width // 2
    plans = [schedule(order, list(range(depth)), gran), schedule(order, swap, gran)]
    me_block = (me_d * q + me_s) // (1 << low)

    def arrange(source, target):
        def turn(c):
            r.turned[span(c, LANES), :] = source[:, span(c, LANES)].astype(F32).T.astype(BF16)

        loop(pairs, turn)
        for u in range(1 << depth):
            block = me_block
            for k, (_, _, place) in enumerate(order):
                if (u >> (depth - 1 - k)) & 1:
                    block = block + (1 - 2 * lax.rem(me_block // (1 << (place - low)), 2)) * (1 << (place - low))
            target[pl.ds(u * gran, gran), :] = r.turned[pl.ds(pl.multiple_of(block * gran, gran), gran), :]

    class Sum:
        def __init__(self, which, left, right):
            self.which, self.left, self.right = which, left, right
            self.total = r.total.at[which]
            self.out, self.arrived = r.sum_out.at[which], r.sum_in.at[which]
            self.k = 0

        def copy(self, part):
            k = self.k
            rows = pl.ds(width - (width >> k), width >> (k + 1))
            cols = pl.ds(part * half_cols, half_cols)
            at = (self.which * 2 + part) * depth + k
            return remote(
                self.out.at[rows, cols],
                self.arrived.at[rows, cols],
                r.sum_send.at[at],
                r.sum_recv.at[at],
                **partner(plans[part][k][0]),
            )

        def begin(self):
            half = width // 2

            def give(i):
                self.out[pl.ds(0, half), span(i, TILE)] = dot(
                    self.left[pl.ds(half, half), :], self.right[:, span(i, TILE)]
                ).astype(BF16)

            loop(tiles, give)
            for part in range(2):
                self.copy(part).start()

            def keep(i):
                self.total[:, span(i, TILE)] = dot(self.left[pl.ds(0, half), :], self.right[:, span(i, TILE)])

            loop(tiles, keep)

        def start(self):
            for part in range(2):
                at = width - (width >> self.k)
                cols = pl.ds(part * half_cols, half_cols)
                for row, size in plans[part][self.k][1]:

                    def put(i, row=row, at=at):
                        self.out[pl.ds(pl.multiple_of(at + i * SUB, SUB), SUB), cols] = self.total[
                            pl.ds(pl.multiple_of(row + i * SUB, SUB), SUB), cols
                        ].astype(BF16)

                    loop(size // SUB, put)
                    at += size
                self.copy(part).start()

        def finish(self):
            for part in range(2):
                self.copy(part).wait()
                at = width - (width >> self.k)
                cols = pl.ds(part * half_cols, half_cols)
                for row, size in plans[part][self.k][2]:

                    def add(i, row=row, at=at):
                        rows = pl.ds(pl.multiple_of(row + i * SUB, SUB), SUB)
                        self.total[rows, cols] = self.total[rows, cols] + self.arrived[
                            pl.ds(pl.multiple_of(at + i * SUB, SUB), SUB), cols
                        ].astype(F32)

                    loop(size // SUB, add)
                    at += size
            self.k += 1

        def step(self):
            if self.k < depth:
                self.finish()
                if self.k < depth:
                    self.start()

    arrange(r.low, r.left_out)
    out_sum = Sum(1, r.left_out, r.g_in)
    out_sum.begin()

    for copy in edge_out:
        copy.wait()
    land(r.halo_out, r.g_pad)

    def back_tile(c):
        at = span(c, LANES)
        own = r.x_pad[c, pl.ds(SUB, frames), :]
        total = jnp.zeros((frames, LANES), F32)
        for tap in range(taps):
            moved = r.g_pad[c, pl.ds(SUB - reach + tap, frames), :] * r.same[tap]
            back = taps - 1 - tap
            total = total + r.taps_f[back : back + 1, at] * moved
            r.tap_sum[back : back + 1, at] = jnp.sum(own * moved, 0, keepdims=True)
        linear, logistic = r.linear[:, at], r.logistic[:, at]
        gated = total * logistic
        r.both_grad[:, at] = gated.astype(BF16)
        r.both_grad[:, span(c + pairs, LANES)] = (gated * linear * (1.0 - logistic)).astype(BF16)

    tap_rows = r.tap_sum.shape[0]
    r.tap_sum[pl.ds(tap_rows - SUB, SUB), :] = jnp.zeros((SUB, width), F32)
    loop(pairs, back_tile)

    everyone = bits_of(n, q)

    def tap_copy(k):
        return remote(
            r.tap_out.at[k], r.tap_in.at[k], r.tap_send.at[k], r.tap_recv.at[k], **partner(everyone[k])
        )

    def tap_start(k):
        rounded = r.tap_sum[...].astype(BF16)
        r.tap_out[k] = rounded
        tap_copy(k).start()

    def tap_finish(k):
        tap_copy(k).wait()
        r.tap_sum[...] = r.tap_out[k].astype(F32) + r.tap_in[k].astype(F32)

    tap_start(0)
    out_sum.step()

    def back_in_tile(i):
        r.work[:, span(i, TILE)] = dot_t(r.both_grad[...], r.pin[span(i, TILE), :])

    loop(tiles, back_in_tile)

    def stream_rows(i):
        at = span(i, SUB)
        hat = r.hat_in[at, :]
        scaled = r.work[at, :] * r.norm_gain[...]
        grad = r.inv_in[at, :][:, :1] * (
            scaled - jnp.mean(scaled, -1, keepdims=True) - hat * jnp.mean(scaled * hat, -1, keepdims=True)
        )
        r.stream_out[at, :] = (r.g_in[at, :].astype(F32) + grad).astype(BF16)

    loop(frames // SUB, stream_rows)
    spread([r.stream_out], r.inter_s, r.route_sem.at[4], r.route_sem.at[5])
    spread_own([r.stream_out], r.inter_s)

    deliver_done(3, r.stage, r.route_sem.at[2], r.route_sem.at[3])
    slot_wide = widen(r.slot, 3, r.wide_send, r.wide_recv)
    for copy in slot_wide:
        copy.start()

    arrange(r.mixed, r.left_in)
    in_sum = Sum(0, r.left_in, r.stream_out)
    in_sum.begin()

    spread_done(1, r.inter_s, r.route_sem.at[4], r.route_sem.at[5])
    deliver(1, r.inter_s, r.stage_s, r.slot_s, r.route_sem.at[6], r.route_sem.at[7])
    tap_finish(0)
    tap_start(1)
    out_sum.step()
    in_sum.step()
    deliver_done(1, r.stage_s, r.route_sem.at[6], r.route_sem.at[7])
    stream_wide = widen(r.slot_s, 1, r.wide_send_s, r.wide_recv_s)
    for copy in stream_wide:
        copy.start()
    tap_finish(1)
    tap_start(2)
    out_sum.step()
    in_sum.step()
    for copy in slot_wide:
        copy.wait()
    for copy in stream_wide:
        copy.wait()
    r.stream_grad[0] = r.slot_s[0, pl.ds(0, frames), :]

    def mixed_tile(i):
        r.mixed_grad[:, span(i, TILE)] = dot_t(r.slot_s[0], r.ao[span(i, TILE), :]).astype(BF16)

    loop(tiles, mixed_tile)

    def back_pair(i):
        at = span(i, LANES)
        key_two, value_two = r.slot[1, :, at], r.slot[2, :, at]

        def block(b):
            rows = span(b, frames)
            queries = stacked(r.slot[0, rows, at], scale)
            grads = stacked(r.mixed_grad[rows, at])
            weights = softmax(dot_t(queries, key_two), r.slot_bias[rows, :])
            slope = dot_t(grads, value_two)
            delta = jnp.sum(weights * slope, -1, keepdims=True)
            score_grad = (weights * (slope - delta)).astype(BF16)
            return (
                score_grad,
                t_dot(score_grad[:, :frames], queries),
                t_dot(weights[:, :frames].astype(BF16), grads),
            )

        score_grad, key_part, value_part = block(0)
        r.query_grad[0, :, at] = (merged(dot(score_grad, key_two)) * scale).astype(BF16)

        def more(b, carry):
            _, key_more, value_more = block(b)
            return carry[0] + key_more, carry[1] + value_more

        key_part, value_part = lax.fori_loop(1, q, more, (key_part, value_part))
        r.key_grad[0, :, at] = key_part.astype(BF16)
        r.value_grad[0, :, at] = value_part.astype(BF16)

    def between(first_pair, count):
        loop(count, lambda i: back_pair(first_pair + i))

    rest = max(len(everyone), depth) - 2
    done = 0
    for k in range(rest):
        until = pairs * (k + 1) // rest
        between(done, until - done)
        done = until
        if k + 2 < len(everyone):
            tap_finish(k + 2)
            if k + 3 < len(everyone):
                tap_start(k + 3)
        out_sum.step()
        in_sum.step()
    while in_sum.k < depth:
        out_sum.step()
        in_sum.step()
    r.kernel_grad[...] = r.tap_sum[pl.ds(0, taps), :]
    r.proj[:, pl.ds(0, width)] = r.total[0, pl.ds(0, gran), :]
    r.proj[:, pl.ds(width, width)] = r.total[1, pl.ds(0, gran), :]


def swapped(cells, axis, bit):
    return lax.ppermute(cells, axis, [(i, i ^ (1 << bit)) for i in range(lax.axis_size(axis))])


def finished(cells, left, low):
    for axis, bit, place in sorted(left, key=lambda e: -e[2]):
        mine = (lax.axis_index(axis) >> bit) & 1
        split = cells.reshape(2, -1, cells.shape[1])
        out = lax.dynamic_index_in_dim(split, 1 - mine, 0, keepdims=False)
        cells = lax.dynamic_index_in_dim(split, mine, 0, keepdims=False) + swapped(
            out.astype(BF16), axis, bit
        ).astype(F32)
    return cells


def per_device(
    queries, keys, values, stream, cotangent, attn_out, point_in, kernel, point_out, norm_gain, conv_gain, segments, plan
):
    n, q = lax.axis_size("dp"), lax.axis_size("seq")
    frames, width = queries.shape[1:]
    taps = kernel.shape[0]
    whole = q * frames
    pairs = width // LANES
    rows_c, cols_c, _ = chunking(n, frames, width)
    order, left, low = split_bits(n, q, width)
    depth = len(order)
    everyone = len(bits_of(n, q))
    parts = width // TILE
    tap_rows = -(-taps // SUB) * SUB
    any_, vmem, smem = (pl.BlockSpec(memory_space=m) for m in (pl.ANY, pltpu.VMEM, pltpu.SMEM))
    ins = dict(
        queries=any_,
        keys=any_,
        values=any_,
        stream=any_,
        cotangent=any_,
        attn_out=any_,
        point_in=any_,
        kernel=vmem,
        point_out=any_,
        norm_gain=vmem,
        conv_gain=vmem,
        segments=vmem,
        plan=smem,
    )
    low_block = jax.ShapeDtypeStruct((1, frames, width), BF16)
    outs = dict(
        query_grad=low_block,
        key_grad=low_block,
        value_grad=low_block,
        stream_grad=low_block,
        kernel_grad=jax.ShapeDtypeStruct((taps, width), F32),
        proj=jax.ShapeDtypeStruct((width >> depth, 2 * width), F32),
    )
    dma = pltpu.SemaphoreType.DMA

    def low_(*shape):
        return pltpu.VMEM(shape, BF16)

    def full_(*shape):
        return pltpu.VMEM(shape, F32)

    padded = frames + 2 * SUB
    scratch = dict(
        g_in=low_(frames, width),
        po=low_(width, width),
        q_in=low_(frames, width),
        x_in=low_(frames, width),
        ao=low_(width, width),
        pin=low_(width, 2 * width),
        k_all=low_(whole, width),
        v_all=low_(whole, width),
        inter=low_(3, n, rows_c, cols_c),
        stage=low_(3, n, rows_c, cols_c),
        slot=low_(3, whole, width),
        inter_s=low_(1, n, rows_c, cols_c),
        stage_s=low_(1, n, rows_c, cols_c),
        slot_s=low_(1, whole, width),
        bias=full_(frames, whole),
        slot_bias=full_(whole, whole),
        id_pad=full_(padded, LANES),
        same=full_(taps, frames, LANES),
        taps_f=full_(tap_rows, width),
        act_grad=full_(frames, width),
        mixed=low_(frames, width),
        hat_in=full_(frames, width),
        inv_in=full_(frames, LANES),
        low=low_(frames, width),
        linear=full_(frames, width),
        logistic=full_(frames, width),
        conv_in=low_(frames, width),
        conv_grad=low_(frames, width),
        x_pad=full_(pairs, padded, LANES),
        g_pad=full_(pairs, padded, LANES),
        halo_in=low_(2, SUB, width),
        halo_out=low_(2, SUB, width),
        work=full_(frames, width),
        turned=low_(width, frames),
        left_out=low_(width, frames),
        left_in=low_(width, frames),
        total=full_(2, width // 2, width),
        sum_out=low_(2, width, width),
        sum_in=low_(2, width, width),
        tap_sum=full_(tap_rows, width),
        tap_out=low_(everyone, tap_rows, width),
        tap_in=low_(everyone, tap_rows, width),
        both_grad=low_(frames, 2 * width),
        stream_out=low_(frames, width),
        mixed_grad=low_(whole, width),
        load_sem=dma((8,)),
        kv_send=dma(((q - 1) * parts * 2,)),
        kv_recv=dma(((q - 1) * parts * 2,)),
        route_sem=dma((8,)),
        wide_send=dma(((q - 1) * 3,)),
        wide_recv=dma(((q - 1) * 3,)),
        wide_send_s=dma((q - 1,)),
        wide_recv_s=dma((q - 1,)),
        edge_send=dma((4,)),
        edge_recv=dma((4,)),
        sum_send=dma((4 * depth,)),
        sum_recv=dma((4 * depth,)),
        tap_send=dma((everyone,)),
        tap_recv=dma((everyone,)),
    )
    names = (*ins, *outs, *scratch)
    query_grad, key_grad, value_grad, stream_grad, kernel_grad, proj = pl.pallas_call(
        functools.partial(body, n, q, names),
        out_shape=tuple(outs.values()),
        in_specs=list(ins.values()),
        out_specs=(vmem,) * len(outs),
        scratch_shapes=list(scratch.values()),
        compiler_params=pltpu.CompilerParams(
            collective_id=0, has_side_effects=True, vmem_limit_bytes=60 * 2**20
        ),
    )(
        queries,
        keys,
        values,
        stream,
        cotangent,
        attn_out,
        point_in,
        kernel,
        point_out,
        norm_gain.reshape(1, width),
        conv_gain.reshape(1, width),
        segments,
        plan,
    )
    return query_grad, key_grad, value_grad, stream_grad, kernel_grad, finished(proj, left, low)


def solution(mesh):
    rows = P("dp", "seq", None)
    return jax.shard_map(
        per_device,
        mesh=mesh,
        in_specs=(rows,) * 5 + (P(),) * 8,
        out_specs=(rows,) * 4 + (P(), P(("dp", "seq"), None)),
        check_vma=False,
    )
```

```python
import functools
import types

import jax
import jax.numpy as jnp
from jax import lax
from jax.experimental import pallas as pl
from jax.experimental.pallas import tpu as pltpu
from jax.sharding import PartitionSpec as P

HEAD_DIM = 64
EPSILON = 1e-05
MASKED = -1e30
LANES = 128
TILE = 256
SUB = 16
KEPT = 8 * 2**20
F32 = jnp.float32
BF16 = jnp.bfloat16


def dot(left, right):
    return jnp.dot(left, right, preferred_element_type=F32)


def dot_t(left, right):
    return lax.dot_general(left, right, (((1,), (1,)), ((), ())), preferred_element_type=F32)


def t_dot(left, right):
    return lax.dot_general(left, right, (((0,), (0,)), ((), ())), preferred_element_type=F32)


def loop(count, body):
    def step(i, carry):
        body(i)
        return carry

    lax.fori_loop(0, count, step, 0)


def span(i, size):
    return pl.ds(pl.multiple_of(i * size, size), size)


def log2(count):
    return (count - 1).bit_length()


def chunking(count, rows, width):
    down = min(count, rows // SUB)
    return rows // down, width // (count // down)


def bits_of(n, q):
    seqs = log2(q)
    return (
        [("dp", bit, seqs + bit) for bit in range(min(1, log2(n)))]
        + [("seq", bit, bit) for bit in range(seqs)]
        + [("dp", bit, seqs + bit) for bit in range(1, log2(n))]
    )


def split_bits(n, q, width):
    low = 0
    while (width >> (log2(n) + log2(q) - low)) < SUB:
        low += 1
    order = bits_of(n, q)
    return [e for e in order if e[2] >= low], [e for e in order if e[2] < low], low


def groups_of(order):
    dps = [e for e in order if e[0] == "dp"]
    return dps[:1], dps[:2]


def runs_of(blocks, rows):
    runs = []
    for block in blocks:
        if runs and runs[-1][0] + runs[-1][1] == block * rows:
            runs[-1][1] += rows
        else:
            runs.append([block * rows, rows])
    return runs


def schedule(order, sequence, rows):
    depth = len(order)
    kept = list(range(1 << depth))
    plan = []
    for which in sequence:
        bit = 1 << (depth - 1 - which)
        plan.append((order[which], runs_of([u for u in kept if u & bit], rows), runs_of([u for u in kept if not u & bit], rows)))
        kept = [u for u in kept if not u & bit]
    return plan


def body(n, q, names, *refs):
    r = types.SimpleNamespace(**dict(zip(names, refs)))
    frames, width = r.x_in.shape
    whole = q * frames
    taps = r.kernel.shape[0]
    reach = taps // 2
    pairs = width // LANES
    parts = width // TILE
    tiles = width // TILE
    me_d, me_s = lax.axis_index("dp"), lax.axis_index("seq")
    scale = HEAD_DIM ** (-0.5)
    order, _, low = split_bits(n, q, width)

    def remote(src, dst, ssem, rsem, dp=None, seq=None):
        return pltpu.make_async_remote_copy(
            src_ref=src,
            dst_ref=dst,
            send_sem=ssem,
            recv_sem=rsem,
            device_id=(me_d if dp is None else dp, me_s if seq is None else seq),
            device_id_type=pl.DeviceIdType.MESH,
        )

    def drain(view, sem):
        pltpu.make_async_copy(view, view, sem).wait()

    def flipped(place, bit):
        mine = lax.rem(place // (1 << bit), 2)
        return place + (1 - 2 * mine) * (1 << bit)

    def partner(entry):
        axis, bit, _ = entry
        if axis == "dp":
            return dict(dp=flipped(me_d, bit))
        return dict(seq=flipped(me_s, bit))

    loads = [
        (r.keys.at[0], r.k_all.at[pl.ds(0, frames)]),
        (r.values.at[0], r.v_all.at[pl.ds(0, frames)]),
        (r.cotangent.at[0], r.g_in),
        (r.point_out, r.po),
        (r.queries.at[0], r.q_in),
        (r.stream.at[0], r.x_in),
        (r.attn_out, r.ao),
        (r.point_in, r.pin),
    ]
    loads = [pltpu.make_async_copy(src, dst, r.load_sem.at[at]) for at, (src, dst) in enumerate(loads)]
    for copy in loads:
        copy.start()
    load_k, load_v, load_g, load_po, load_q, load_x, load_ao, load_pin = loads

    barrier = pltpu.get_barrier_semaphore()

    def greet_dp(step):
        pl.semaphore_signal(
            barrier, inc=1, device_id=(lax.rem(me_d + 1 + step, n), me_s), device_id_type=pl.DeviceIdType.MESH
        )

    def greet_seq(step):
        pl.semaphore_signal(
            barrier, inc=1, device_id=(me_d, lax.rem(me_s + 1 + step, q)), device_id_type=pl.DeviceIdType.MESH
        )

    loop(n - 1, greet_dp)
    loop(q - 1, greet_seq)
    pl.semaphore_wait(barrier, n + q - 2)

    def pair_copy(which, step, part):
        source, target = ((r.keys, r.k_all), (r.values, r.v_all))[which]
        at = ((step - 1) * parts + part) * 2 + which
        return remote(
            source.at[0, :, span(part, TILE)],
            target.at[pl.ds(step * frames, frames), span(part, TILE)],
            r.kv_send.at[at],
            r.kv_recv.at[at],
            seq=lax.rem(me_s + q - step, q),
        )

    def send_part(part):
        for step in range(1, q):
            for which in range(2):
                pair_copy(which, step, part).start()

    loop(parts, send_part)

    def sems(k):
        return r.route_sem.at[2 * k], r.route_sem.at[2 * k + 1]

    def piece(place, inter):
        rows, cols = inter.shape[1:]
        across = n // (frames // rows)
        return (
            pl.ds(pl.multiple_of((place // across) * rows, rows), rows),
            pl.ds(pl.multiple_of(lax.rem(place, across) * cols, cols), cols),
        )

    def spread(source, inter, k):
        ssem, rsem = sems(k)

        def send(step):
            to = lax.rem(me_d + 1 + step, n)
            at = piece(to, inter)
            remote(source.at[at[0], at[1]], inter.at[me_d], ssem, rsem, dp=to).start()

        loop(n - 1, send)

    def spread_own(source, inter):
        at = piece(me_d, inter)
        inter[me_d] = source[at[0], at[1]]

    def settle(view, k):
        ssem, rsem = sems(k)
        view = view.at[pl.ds(0, n - 1)]
        drain(view, rsem)
        drain(view, ssem)

    def deliver(inter, stage, target, k):
        ssem, rsem = sems(k)
        at = piece(me_d, inter)

        def send(step):
            to = lax.rem(me_d + 1 + step, n)
            stage[to] = inter[r.plan[to]]
            remote(stage.at[to], target.at[at[0], at[1]], ssem, rsem, dp=to).start()

        loop(n - 1, send)
        target[at[0], at[1]] = inter[r.plan[me_d]]

    def widen(target, ssem, rsem, first_sem):
        return [
            remote(
                target.at[pl.ds(0, frames)],
                target.at[pl.ds(step * frames, frames)],
                ssem.at[first_sem + step - 1],
                rsem.at[first_sem + step - 1],
                seq=lax.rem(me_s + q - step, q),
            )
            for step in range(1, q)
        ]

    def start(copies):
        for copy in copies:
            copy.start()

    def wait(copies):
        for copy in copies:
            copy.wait()

    half_cols = width // 2
    me_block = (me_d * q + me_s) // (1 << low)
    gran = width >> len(order)

    def away(entries, v):
        place = dict(dp=me_d, seq=me_s)
        for k, (axis, bit, _) in enumerate(entries):
            if (v >> k) & 1:
                place[axis] = flipped(place[axis], bit)
        return place

    class Sum:
        def __init__(self, group, sequences, refs):
            self.group, self.rest = group, [e for e in order if e not in group]
            self.members, self.depth = 1 << len(group), len(self.rest)
            self.plans = [schedule(self.rest, sequence, gran) for sequence in sequences]
            self.cols = width // len(sequences)
            (self.left, self.right, self.staged, self.total, self.out, self.arrived, self.swap_sem, self.sum_sem) = refs
            self.rows = self.total.shape[0]
            self.k = 0

        def swap(self, side, v):
            rows = pl.ds(v * frames, frames)
            source, target = ((self.staged.at[v - 1], self.left.at[:, rows]), (self.right.at[pl.ds(0, frames)], self.right.at[rows]))[side]
            at = 2 * v + side
            return remote(source, target, self.swap_sem.at[0, at], self.swap_sem.at[1, at], **away(self.group, v))

        def give_right(self):
            for v in range(1, self.members):
                self.swap(1, v).start()

        def give_left(self, source):
            def turn(c):
                r.turned[span(c, LANES), :] = source[:, span(c, LANES)].astype(F32).T.astype(BF16)

            loop(pairs, turn)
            for v in reversed(range(self.members)):
                for w in range(1 << self.depth):
                    block = me_block
                    flips = [e for k, e in enumerate(self.group) if (v >> k) & 1]
                    flips += [e for k, e in enumerate(self.rest) if (w >> (self.depth - 1 - k)) & 1]
                    for _, _, place in flips:
                        step = 1 << (place - low)
                        block = block + (1 - 2 * lax.rem(me_block // step, 2)) * step
                    piece_ = r.turned[pl.ds(pl.multiple_of(block * gran, gran), gran), :]
                    if v:
                        self.staged[v - 1, pl.ds(w * gran, gran), :] = piece_
                    else:
                        self.left[pl.ds(w * gran, gran), pl.ds(0, frames)] = piece_
                if v:
                    self.swap(0, v).start()

        def multiply(self):
            for v in range(1, self.members):
                self.swap(0, v).wait()
                self.swap(1, v).wait()

            def tile(i):
                self.total[:, span(i, TILE)] = dot(self.left[...], self.right[:, span(i, TILE)])

            loop(tiles, tile)
            self.start()

        def copy(self, part):
            rows = pl.ds(self.rows - (self.rows >> self.k), self.rows >> (self.k + 1))
            cols = pl.ds(part * self.cols, self.cols)
            at = part * self.depth + self.k
            return remote(
                self.out.at[rows, cols],
                self.arrived.at[rows, cols],
                self.sum_sem.at[0, at],
                self.sum_sem.at[1, at],
                **partner(self.plans[part][self.k][0]),
            )

        def start(self):
            for part, plan in enumerate(self.plans):
                at = self.rows - (self.rows >> self.k)
                cols = pl.ds(part * self.cols, self.cols)
                for row, size in plan[self.k][1]:

                    def put(i, row=row, at=at, cols=cols):
                        self.out[pl.ds(pl.multiple_of(at + i * SUB, SUB), SUB), cols] = self.total[
                            pl.ds(pl.multiple_of(row + i * SUB, SUB), SUB), cols
                        ].astype(BF16)

                    loop(size // SUB, put)
                    at += size
                self.copy(part).start()

        def finish(self):
            for part, plan in enumerate(self.plans):
                self.copy(part).wait()
                at = self.rows - (self.rows >> self.k)
                cols = pl.ds(part * self.cols, self.cols)
                for row, size in plan[self.k][2]:

                    def add(i, row=row, at=at, cols=cols):
                        rows = pl.ds(pl.multiple_of(row + i * SUB, SUB), SUB)
                        self.total[rows, cols] = self.total[rows, cols] + self.arrived[
                            pl.ds(pl.multiple_of(at + i * SUB, SUB), SUB), cols
                        ].astype(F32)

                    loop(size // SUB, add)
                    at += size
            self.k += 1

        def step(self):
            if self.k < self.depth:
                self.finish()
                if self.k < self.depth:
                    self.start()

    in_group, out_group = groups_of(order)
    in_rest = list(range(len(order) - len(in_group)))
    seqs = len([e for e in order if e[0] == "seq"])
    swap_rest = [seqs] + in_rest[:seqs] + in_rest[seqs + 1 :] if seqs < len(in_rest) else in_rest
    in_sum = Sum(
        in_group,
        [in_rest, swap_rest],
        (r.in_left, r.in_right, r.in_staged, r.in_total, r.in_out, r.in_in, r.in_swap, r.in_sum),
    )
    out_sum = Sum(
        out_group,
        [list(range(len(order) - len(out_group)))],
        (r.out_left, r.out_right, r.out_staged, r.out_total, r.out_out, r.out_in, r.out_swap, r.out_sum),
    )

    inters = [r.inter_q, r.inter_k, r.inter_v]
    stages = [r.stage.at[a] for a in range(3)]
    slots = [r.slot.at[a] for a in range(3)]
    for a, source in enumerate((r.queries.at[0], r.keys.at[0], r.values.at[0])):
        spread(source, inters[a], a)

    load_g.wait()
    r.out_right[pl.ds(0, frames), :] = r.g_in[...]
    out_sum.give_right()

    def onward(a):
        settle(inters[a], a)
        deliver(inters[a], stages[a], slots[a], 3 + a)

    wide = [widen(slots[a], r.wide_send, r.wide_recv, (q - 1) * a) for a in range(3)]

    def outward(a):
        settle(stages[a], 3 + a)
        start(wide[a])

    def row_ids(row, step):
        block = lax.rem(me_s + step + q, q)
        line = r.segments[pl.ds(row, 1), :]
        chosen = line[:, :frames]
        for b in range(1, q):
            chosen = jnp.where(block == b, line[:, b * frames : (b + 1) * frames], chosen)
        return chosen.astype(F32)

    def col_ids(row, step):
        return jnp.broadcast_to(row_ids(row, step), (LANES, frames)).T

    own_col = col_ids(me_d, 0)
    for step in range(q):
        r.bias[:, pl.ds(step * frames, frames)] = jnp.where(own_col[:, :1] == row_ids(me_d, step), 0.0, MASKED)
    before = jnp.where(me_s > 0, col_ids(me_d, -1)[frames - SUB :], -1.0)
    after = jnp.where(me_s < q - 1, col_ids(me_d, 1)[:SUB], -1.0)
    r.id_pad[pl.ds(0, SUB)] = before
    r.id_pad[pl.ds(SUB, frames)] = own_col
    r.id_pad[pl.ds(SUB + frames, SUB)] = after
    for tap in range(taps):
        r.same[tap] = jnp.where(r.id_pad[pl.ds(SUB - reach + tap, frames)] == own_col, 1.0, 0.0)
    r.taps_f[pl.ds(0, taps)] = r.kernel[...].astype(F32)
    slot_pack = r.plan[me_d]
    for b in range(q):
        col = col_ids(slot_pack, b)
        for step in range(q):
            r.slot_bias[pl.ds(b * frames, frames), pl.ds(step * frames, frames)] = jnp.where(
                col[:, :1] == row_ids(slot_pack, step), 0.0, MASKED
            )

    load_po.wait()

    def act_tile(i):
        r.act_grad[:, span(i, TILE)] = dot_t(r.g_in[...], r.po[span(i, TILE), :])

    loop(tiles, act_tile)

    lane = lax.broadcasted_iota(jnp.int32, (1, LANES), 1)
    first = jnp.where(lane < HEAD_DIM, 1.0, 0.0)
    heads_low = (first.astype(BF16), (1.0 - first).astype(BF16))

    def stacked(two, factor=1.0):
        return jnp.concatenate([two * (h * factor).astype(BF16) for h in heads_low], 0)

    def merged(tall):
        return jnp.where(lane < HEAD_DIM, tall[:frames], tall[frames:])

    def softmax(scores, bias):
        scores = scores + jnp.concatenate([bias, bias], 0)
        raised = jnp.exp(scores - jnp.max(scores, -1, keepdims=True))
        return raised * (1.0 / jnp.sum(raised, -1, keepdims=True))

    load_q.wait()
    load_k.wait()
    load_v.wait()
    for a, source in enumerate((r.q_in, r.k_all, r.v_all)):
        spread_own(source, inters[a])

    def attend_part(part):
        for step in range(1, q):
            for which in range(2):
                pair_copy(which, step, part).wait()

        def attend(i):
            at = span(part * (TILE // LANES) + i, LANES)
            weights = softmax(dot_t(stacked(r.q_in[:, at], scale), r.k_all[:, at]), r.bias[...])
            r.mixed[:, at] = merged(dot(weights.astype(BF16), r.v_all[:, at])).astype(BF16)

        loop(TILE // LANES, attend)

    loop(parts - 1, attend_part)
    onward(0)
    attend_part(parts - 1)
    onward(1)

    load_x.wait()
    load_ao.wait()

    def hidden_tile(i):
        at = span(i, TILE)
        r.hat_in[:, at] = r.x_in[:, at].astype(F32) + dot(r.mixed[...], r.ao[:, at])

    loop(tiles, hidden_tile)

    def norm_rows(i):
        at = span(i, SUB)
        hidden = r.hat_in[at, :]
        shifted = hidden - jnp.mean(hidden, -1, keepdims=True)
        inverse = lax.rsqrt(jnp.mean(shifted * shifted, -1, keepdims=True) + EPSILON)
        normed = shifted * inverse
        r.hat_in[at, :] = normed
        r.inv_in[at, :] = jnp.broadcast_to(inverse, (SUB, LANES))
        r.low[at, :] = (normed * r.norm_gain[...]).astype(BF16)

    loop(frames // SUB, norm_rows)
    load_pin.wait()

    def gate_tile(i):
        at = span(i, TILE)
        linear = dot(r.low[...], r.pin[:, at])
        logistic = jax.nn.sigmoid(dot(r.low[...], r.pin[:, span(i + tiles, TILE)]))
        conv_in = (linear * logistic).astype(BF16)
        r.linear[:, at] = linear
        r.logistic[:, at] = logistic
        r.conv_in[:, at] = conv_in
        wide = conv_in.astype(F32)
        for c in range(TILE // LANES):
            r.x_pad[i * (TILE // LANES) + c, pl.ds(SUB, frames), :] = wide[:, c * LANES : (c + 1) * LANES]

    loop(tiles, gate_tile)

    def edges(source, halo, at):
        return (
            remote(
                source.at[pl.ds(frames - SUB, SUB)],
                halo.at[0],
                r.edge_send.at[at],
                r.edge_recv.at[at],
                seq=lax.rem(me_s + 1, q),
            ),
            remote(
                source.at[pl.ds(0, SUB)],
                halo.at[1],
                r.edge_send.at[at + 1],
                r.edge_recv.at[at + 1],
                seq=lax.rem(me_s + q - 1, q),
            ),
        )

    def land(halo, pad):
        def put(c):
            at = span(c, LANES)
            pad[c, pl.ds(0, SUB), :] = halo[0, :, at].astype(F32)
            pad[c, pl.ds(SUB + frames, SUB), :] = halo[1, :, at].astype(F32)

        loop(pairs, put)

    edge_in = edges(r.conv_in, r.halo_in, 0)
    for copy in edge_in:
        copy.start()

    onward(2)
    in_sum.give_left(r.mixed)

    for copy in edge_in:
        copy.wait()
    land(r.halo_in, r.x_pad)

    def conv_tile(c):
        total = jnp.zeros((frames, LANES), F32)
        for tap in range(taps):
            moved = r.x_pad[c, pl.ds(SUB - reach + tap, frames), :] * r.same[tap]
            total = total + r.taps_f[tap : tap + 1, span(c, LANES)] * moved
        r.work[:, span(c, LANES)] = total

    loop(pairs, conv_tile)

    def mid_rows(i):
        at = span(i, SUB)
        conv = r.work[at, :]
        shifted = conv - jnp.mean(conv, -1, keepdims=True)
        inverse = lax.rsqrt(jnp.mean(shifted * shifted, -1, keepdims=True) + EPSILON)
        hat = shifted * inverse
        gain = r.conv_gain[...]
        normed = hat * gain
        logistic = jax.nn.sigmoid(normed)
        r.low[at, :] = (normed * logistic).astype(BF16)
        scaled = r.act_grad[at, :] * (logistic * (1.0 + normed * (1.0 - logistic))) * gain
        grad = inverse * (
            scaled - jnp.mean(scaled, -1, keepdims=True) - hat * jnp.mean(scaled * hat, -1, keepdims=True)
        )
        r.conv_grad[at, :] = grad.astype(BF16)
        for c in range(pairs):
            r.g_pad[c, pl.ds(pl.multiple_of(i * SUB + SUB, SUB), SUB), :] = grad[:, c * LANES : (c + 1) * LANES]

    loop(frames // SUB, mid_rows)
    edge_out = edges(r.conv_grad, r.halo_out, 2)
    for copy in edge_out:
        copy.start()

    out_sum.give_left(r.low)
    outward(0)

    for copy in edge_out:
        copy.wait()
    land(r.halo_out, r.g_pad)

    def back_tile(c):
        at = span(c, LANES)
        own = r.x_pad[c, pl.ds(SUB, frames), :]
        total = jnp.zeros((frames, LANES), F32)
        for tap in range(taps):
            moved = r.g_pad[c, pl.ds(SUB - reach + tap, frames), :] * r.same[tap]
            back = taps - 1 - tap
            total = total + r.taps_f[back : back + 1, at] * moved
            r.tap_sum[back : back + 1, at] = jnp.sum(own * moved, 0, keepdims=True)
        linear, logistic = r.linear[:, at], r.logistic[:, at]
        gated = total * logistic
        r.both_grad[:, at] = gated.astype(BF16)
        r.both_grad[:, span(c + pairs, LANES)] = (gated * linear * (1.0 - logistic)).astype(BF16)

    tap_rows = r.tap_sum.shape[0]
    r.tap_sum[pl.ds(tap_rows - SUB, SUB), :] = jnp.zeros((SUB, width), F32)
    loop(pairs, back_tile)

    everyone = bits_of(n, q)

    def tap_copy(k):
        return remote(
            r.tap_out.at[k], r.tap_in.at[k], r.tap_send.at[k], r.tap_recv.at[k], **partner(everyone[k])
        )

    def tap_start(k):
        rounded = r.tap_sum[...].astype(BF16)
        r.tap_out[k] = rounded
        tap_copy(k).start()

    def tap_finish(k):
        tap_copy(k).wait()
        r.tap_sum[...] = r.tap_out[k].astype(F32) + r.tap_in[k].astype(F32)

    tap_at = [0]

    def tap_next():
        if tap_at[0] < len(everyone):
            tap_finish(tap_at[0])
            tap_at[0] += 1
            if tap_at[0] < len(everyone):
                tap_start(tap_at[0])

    tap_start(0)
    outward(1)
    out_sum.multiply()

    def back_in_tile(i):
        r.work[:, span(i, TILE)] = dot_t(r.both_grad[...], r.pin[span(i, TILE), :])

    tap_next()
    loop(tiles, back_in_tile)

    def stream_rows(i):
        at = span(i, SUB)
        hat = r.hat_in[at, :]
        scaled = r.work[at, :] * r.norm_gain[...]
        grad = r.inv_in[at, :][:, :1] * (
            scaled - jnp.mean(scaled, -1, keepdims=True) - hat * jnp.mean(scaled * hat, -1, keepdims=True)
        )
        done = (r.g_in[at, :].astype(F32) + grad).astype(BF16)
        r.in_right[at, :] = done
        for h in range(2):
            r.stream_two[h, at, :] = done[:, h * half_cols : (h + 1) * half_cols]

    loop(frames // SUB, stream_rows)
    twos = [r.stream_two.at[h] for h in range(2)]
    inters_s = [r.inter_a, r.inter_b]
    stages_s = [r.stage_s.at[h] for h in range(2)]
    slots_s = [r.slot_s.at[h] for h in range(2)]
    wide_s = [widen(slots_s[h], r.wide_send_s, r.wide_recv_s, (q - 1) * h) for h in range(2)]
    for h in range(2):
        spread(twos[h], inters_s[h], 6 + h)
    for h in range(2):
        spread_own(twos[h], inters_s[h])
    in_sum.give_right()
    tap_next()
    out_sum.step()
    in_sum.multiply()

    def pass_on(h):
        settle(inters_s[h], 6 + h)
        deliver(inters_s[h], stages_s[h], slots_s[h], 8 + h)

    def pass_wide(h):
        settle(stages_s[h], 8 + h)
        start(wide_s[h])

    def slot_weights(i, b):
        rows, at = span(b, frames), span(i, LANES)
        queries = stacked(r.slot[0, rows, at], scale)
        return softmax(dot_t(queries, r.slot[1, :, at]), r.slot_bias[rows, :])

    def weigh(first_pair, count):
        if r.kept.shape[0] < pairs:
            return

        def one(i):
            def of_block(b):
                r.kept[first_pair + i, b] = slot_weights(first_pair + i, b)

            loop(q, of_block)

        loop(count, one)

    pass_on(0)
    outward(2)
    tap_next()
    pass_on(1)
    out_sum.step()
    wait(wide[0])
    wait(wide[1])
    weigh(0, pairs // 2)
    tap_next()
    in_sum.step()
    pass_wide(0)
    weigh(pairs // 2, pairs - pairs // 2)
    pass_wide(1)
    tap_next()
    out_sum.step()
    in_sum.step()
    wait(wide[2])
    wait(wide_s[0])
    wait(wide_s[1])
    for h in range(2):
        r.stream_grad[0, :, pl.ds(h * half_cols, half_cols)] = r.slot_s[h, pl.ds(0, frames), :]

    def mixed_tile(i):
        r.mixed_grad[:, span(i, TILE)] = (
            dot_t(r.slot_s[0], r.ao[span(i, TILE), pl.ds(0, half_cols)])
            + dot_t(r.slot_s[1], r.ao[span(i, TILE), pl.ds(half_cols, half_cols)])
        ).astype(BF16)

    loop(tiles, mixed_tile)

    def back_pair(i):
        at = span(i, LANES)
        key_two, value_two = r.slot[1, :, at], r.slot[2, :, at]

        def block(b):
            rows = span(b, frames)
            queries = stacked(r.slot[0, rows, at], scale)
            grads = stacked(r.mixed_grad[rows, at])
            weights = r.kept[i, b] if r.kept.shape[0] == pairs else slot_weights(i, b)
            slope = dot_t(grads, value_two)
            delta = jnp.sum(weights * slope, -1, keepdims=True)
            score_grad = (weights * (slope - delta)).astype(BF16)
            return (
                score_grad,
                t_dot(score_grad[:, :frames], queries),
                t_dot(weights[:, :frames].astype(BF16), grads),
            )

        score_grad, key_part, value_part = block(0)
        r.query_grad[0, :, at] = (merged(dot(score_grad, key_two)) * scale).astype(BF16)

        def more(b, carry):
            _, key_more, value_more = block(b)
            return carry[0] + key_more, carry[1] + value_more

        key_part, value_part = lax.fori_loop(1, q, more, (key_part, value_part))
        r.key_grad[0, :, at] = key_part.astype(BF16)
        r.value_grad[0, :, at] = value_part.astype(BF16)

    def between(first_pair, count):
        loop(count, lambda i: back_pair(first_pair + i))

    rest = max(in_sum.depth - in_sum.k, 1)
    done = 0
    for k in range(rest):
        until = pairs * (k + 1) // rest
        between(done, until - done)
        done = until
        out_sum.step()
        in_sum.step()
    while tap_at[0] < len(everyone):
        tap_next()
    while max(in_sum.depth - in_sum.k, out_sum.depth - out_sum.k) > 0:
        out_sum.step()
        in_sum.step()
    r.kernel_grad[...] = r.tap_sum[pl.ds(0, taps), :]
    r.proj[:, pl.ds(0, width)] = r.in_total[pl.ds(0, gran), :]
    r.proj[:, pl.ds(width, width)] = r.out_total[pl.ds(0, gran), :]


def handed_out(*refs):
    count = len(refs) // 2
    for i in range(count):
        refs[count + i][...] = refs[i][...]


def swapped(cells, axis, bit):
    return lax.ppermute(cells, axis, [(i, i ^ (1 << bit)) for i in range(lax.axis_size(axis))])


def finished(cells, left, low):
    for axis, bit, place in sorted(left, key=lambda e: -e[2]):
        mine = (lax.axis_index(axis) >> bit) & 1
        split = cells.reshape(2, -1, cells.shape[1])
        out = lax.dynamic_index_in_dim(split, 1 - mine, 0, keepdims=False)
        cells = lax.dynamic_index_in_dim(split, mine, 0, keepdims=False) + swapped(
            out.astype(BF16), axis, bit
        ).astype(F32)
    return cells


def per_device(
    queries, keys, values, stream, cotangent, attn_out, point_in, kernel, point_out, norm_gain, conv_gain, segments, plan
):
    n, q = lax.axis_size("dp"), lax.axis_size("seq")
    frames, width = queries.shape[1:]
    taps = kernel.shape[0]
    whole = q * frames
    pairs = width // LANES
    rows_c, cols_c = chunking(n, frames, width)
    rows_s, cols_s = chunking(n, frames, width // 2)
    keep = pairs * q * 2 * frames * whole * 4 <= KEPT
    order, left, low = split_bits(n, q, width)
    depth = len(order)
    everyone = len(bits_of(n, q))
    parts = width // TILE
    tap_rows = -(-taps // SUB) * SUB
    any_, vmem, smem = (pl.BlockSpec(memory_space=m) for m in (pl.ANY, pltpu.VMEM, pltpu.SMEM))
    ins = dict(
        queries=any_,
        keys=any_,
        values=any_,
        stream=any_,
        cotangent=any_,
        attn_out=any_,
        point_in=any_,
        kernel=vmem,
        point_out=any_,
        norm_gain=vmem,
        conv_gain=vmem,
        segments=vmem,
        plan=smem,
    )
    low_block = jax.ShapeDtypeStruct((1, frames, width), BF16)
    outs = dict(
        query_grad=low_block,
        key_grad=low_block,
        value_grad=low_block,
        stream_grad=low_block,
        kernel_grad=jax.ShapeDtypeStruct((taps, width), F32),
        proj=jax.ShapeDtypeStruct((width >> depth, 2 * width), F32),
    )
    dma = pltpu.SemaphoreType.DMA

    def low_(*shape):
        return pltpu.VMEM(shape, BF16)

    def full_(*shape):
        return pltpu.VMEM(shape, F32)

    padded = frames + 2 * SUB
    sums = {}
    for name, group, sequences in zip(("in_", "out_"), groups_of(order), (2, 1)):
        members, rows = 1 << len(group), width >> len(group)
        made = dict(
            left=low_(rows, members * frames),
            right=low_(members * frames, width),
            staged=low_(members - 1, rows, frames),
            total=full_(rows, width),
            out=low_(rows, width),
            swap=dma((2, 2 * members)),
            sum=dma((2, sequences * (depth - len(group)))),
        )
        made.update({"in": low_(rows, width)})
        sums.update({name + key: value for key, value in made.items()})
    scratch = dict(
        g_in=low_(frames, width),
        po=low_(width, width),
        q_in=low_(frames, width),
        x_in=low_(frames, width),
        ao=low_(width, width),
        pin=low_(width, 2 * width),
        k_all=low_(whole, width),
        v_all=low_(whole, width),
        inter_q=low_(n, rows_c, cols_c),
        inter_k=low_(n, rows_c, cols_c),
        inter_v=low_(n, rows_c, cols_c),
        stage=low_(3, n, rows_c, cols_c),
        slot=low_(3, whole, width),
        inter_a=low_(n, rows_s, cols_s),
        inter_b=low_(n, rows_s, cols_s),
        stage_s=low_(2, n, rows_s, cols_s),
        slot_s=low_(2, whole, width // 2),
        kept=full_(pairs if keep else 1, q, 2 * frames, whole),
        bias=full_(frames, whole),
        slot_bias=full_(whole, whole),
        id_pad=full_(padded, LANES),
        same=full_(taps, frames, LANES),
        taps_f=full_(tap_rows, width),
        act_grad=full_(frames, width),
        mixed=low_(frames, width),
        hat_in=full_(frames, width),
        inv_in=full_(frames, LANES),
        low=low_(frames, width),
        linear=full_(frames, width),
        logistic=full_(frames, width),
        conv_in=low_(frames, width),
        conv_grad=low_(frames, width),
        x_pad=full_(pairs, padded, LANES),
        g_pad=full_(pairs, padded, LANES),
        halo_in=low_(2, SUB, width),
        halo_out=low_(2, SUB, width),
        work=full_(frames, width),
        turned=low_(width, frames),
        **sums,
        tap_sum=full_(tap_rows, width),
        tap_out=low_(everyone, tap_rows, width),
        tap_in=low_(everyone, tap_rows, width),
        both_grad=low_(frames, 2 * width),
        stream_two=low_(2, frames, width // 2),
        mixed_grad=low_(whole, width),
        load_sem=dma((8,)),
        kv_send=dma(((q - 1) * parts * 2,)),
        kv_recv=dma(((q - 1) * parts * 2,)),
        route_sem=dma((20,)),
        wide_send=dma(((q - 1) * 3,)),
        wide_recv=dma(((q - 1) * 3,)),
        wide_send_s=dma((2 * (q - 1),)),
        wide_recv_s=dma((2 * (q - 1),)),
        edge_send=dma((4,)),
        edge_recv=dma((4,)),
        tap_send=dma((everyone,)),
        tap_recv=dma((everyone,)),
    )
    names = (*ins, *outs, *scratch)
    query_grad, key_grad, value_grad, stream_grad, kernel_grad, proj = pl.pallas_call(
        functools.partial(body, n, q, names),
        out_shape=tuple(outs.values()),
        in_specs=list(ins.values()),
        out_specs=(vmem,) * len(outs),
        scratch_shapes=list(scratch.values()),
        compiler_params=pltpu.CompilerParams(
            collective_id=0, has_side_effects=True, vmem_limit_bytes=60 * 2**20
        ),
    )(
        queries,
        keys,
        values,
        stream,
        cotangent,
        attn_out,
        point_in,
        kernel,
        point_out,
        norm_gain.reshape(1, width),
        conv_gain.reshape(1, width),
        segments,
        plan,
    )
    results = (query_grad, key_grad, value_grad, stream_grad, kernel_grad, finished(proj, left, low))
    return pl.pallas_call(
        handed_out,
        out_shape=tuple(jax.ShapeDtypeStruct(x.shape, x.dtype) for x in results),
        in_specs=[vmem] * len(results),
        out_specs=(vmem,) * len(results),
    )(*results)


def solution(mesh):
    rows = P("dp", "seq", None)
    return jax.shard_map(
        per_device,
        mesh=mesh,
        in_specs=(rows,) * 5 + (P(),) * 8,
        out_specs=(rows,) * 4 + (P(), P(("dp", "seq"), None)),
        check_vma=False,
    )
```

```python
import functools
import types

import jax
import jax.numpy as jnp
from jax import lax
from jax.experimental import pallas as pl
from jax.experimental.pallas import tpu as pltpu
from jax.sharding import PartitionSpec as P

HEAD_DIM = 64
EPSILON = 1e-05
MASKED = -1e30
LANES = 128
TILE = 256
SUB = 16
KEPT = 8 * 2**20
F32 = jnp.float32
BF16 = jnp.bfloat16


def dot(left, right):
    return jnp.dot(left, right, preferred_element_type=F32)


def dot_t(left, right):
    return lax.dot_general(left, right, (((1,), (1,)), ((), ())), preferred_element_type=F32)


def t_dot(left, right):
    return lax.dot_general(left, right, (((0,), (0,)), ((), ())), preferred_element_type=F32)


def loop(count, body):
    def step(i, carry):
        body(i)
        return carry

    lax.fori_loop(0, count, step, 0)


def span(i, size):
    if isinstance(i, int):
        return pl.ds(i * size, size)
    return pl.ds(pl.multiple_of(i * size, size), size)


def rows_loop(count, body):
    for i in range(count):
        body(i)


def log2(count):
    return (count - 1).bit_length()


def chunking(count, rows, width):
    down = min(count, rows // SUB)
    return rows // down, width // (count // down)


def bits_of(n, q):
    seqs = log2(q)
    return (
        [("dp", bit, seqs + bit) for bit in range(min(1, log2(n)))]
        + [("seq", bit, bit) for bit in range(seqs)]
        + [("dp", bit, seqs + bit) for bit in range(1, log2(n))]
    )


def split_bits(n, q, width):
    low = 0
    while (width >> (log2(n) + log2(q) - low)) < SUB:
        low += 1
    order = bits_of(n, q)
    return [e for e in order if e[2] >= low], [e for e in order if e[2] < low], low


def groups_of(order):
    dps = [e for e in order if e[0] == "dp"]
    return dps[:1], dps[:1] + [e for e in order if e[0] == "seq"]


def runs_of(blocks, rows):
    runs = []
    for block in blocks:
        if runs and runs[-1][0] + runs[-1][1] == block * rows:
            runs[-1][1] += rows
        else:
            runs.append([block * rows, rows])
    return runs


def schedule(order, sequence, rows):
    depth = len(order)
    kept = list(range(1 << depth))
    plan = []
    for which in sequence:
        bit = 1 << (depth - 1 - which)
        plan.append((order[which], runs_of([u for u in kept if u & bit], rows), runs_of([u for u in kept if not u & bit], rows)))
        kept = [u for u in kept if not u & bit]
    return plan


def body(n, q, names, *refs):
    r = types.SimpleNamespace(**dict(zip(names, refs)))
    frames, width = r.x_in.shape
    whole = q * frames
    taps = r.kernel.shape[0]
    reach = taps // 2
    pairs = width // LANES
    parts = width // TILE
    tiles = width // TILE
    me_d, me_s = lax.axis_index("dp"), lax.axis_index("seq")
    scale = HEAD_DIM ** (-0.5)
    order, _, low = split_bits(n, q, width)

    def remote(src, dst, ssem, rsem, dp=None, seq=None):
        return pltpu.make_async_remote_copy(
            src_ref=src,
            dst_ref=dst,
            send_sem=ssem,
            recv_sem=rsem,
            device_id=(me_d if dp is None else dp, me_s if seq is None else seq),
            device_id_type=pl.DeviceIdType.MESH,
        )

    def drain(view, sem):
        pltpu.make_async_copy(view, view, sem).wait()

    def flipped(place, bit):
        mine = lax.rem(place // (1 << bit), 2)
        return place + (1 - 2 * mine) * (1 << bit)

    def partner(entry):
        axis, bit, _ = entry
        if axis == "dp":
            return dict(dp=flipped(me_d, bit))
        return dict(seq=flipped(me_s, bit))

    loads = [
        (r.keys.at[0], r.k_all.at[pl.ds(0, frames)]),
        (r.values.at[0], r.v_all.at[pl.ds(0, frames)]),
        (r.cotangent.at[0], r.g_in),
        (r.point_out, r.po),
        (r.queries.at[0], r.q_in),
        (r.stream.at[0], r.x_in),
        (r.attn_out, r.ao),
        (r.point_in, r.pin),
    ]
    loads = [pltpu.make_async_copy(src, dst, r.load_sem.at[at]) for at, (src, dst) in enumerate(loads)]
    for copy in loads:
        copy.start()
    load_k, load_v, load_g, load_po, load_q, load_x, load_ao, load_pin = loads

    def away(entries, v):
        place = dict(dp=me_d, seq=me_s)
        for k, (axis, bit, _) in enumerate(entries):
            if (v >> k) & 1:
                place[axis] = flipped(place[axis], bit)
        return place

    barrier = pltpu.get_barrier_semaphore()

    def greet_dp(step):
        pl.semaphore_signal(
            barrier, inc=1, device_id=(lax.rem(me_d + 1 + step, n), me_s), device_id_type=pl.DeviceIdType.MESH
        )

    def greet_seq(step):
        pl.semaphore_signal(
            barrier, inc=1, device_id=(me_d, lax.rem(me_s + 1 + step, q)), device_id_type=pl.DeviceIdType.MESH
        )

    loop(n - 1, greet_dp)
    loop(q - 1, greet_seq)
    in_group, out_group = groups_of(order)
    across = [
        v
        for v in range(1 << len(out_group))
        if len({axis for k, (axis, _, _) in enumerate(out_group) if (v >> k) & 1}) > 1
    ]
    for v in across:
        far = away(out_group, v)
        pl.semaphore_signal(barrier, inc=1, device_id=(far["dp"], far["seq"]), device_id_type=pl.DeviceIdType.MESH)
    pl.semaphore_wait(barrier, n + q - 2 + len(across))

    def pair_copy(which, step, part):
        source, target = ((r.keys, r.k_all), (r.values, r.v_all))[which]
        at = ((step - 1) * parts + part) * 2 + which
        return remote(
            source.at[0, :, span(part, TILE)],
            target.at[pl.ds(step * frames, frames), span(part, TILE)],
            r.kv_send.at[at],
            r.kv_recv.at[at],
            seq=lax.rem(me_s + q - step, q),
        )

    def send_part(part):
        for step in range(1, q):
            for which in range(2):
                pair_copy(which, step, part).start()

    loop(parts, send_part)

    def sems(k):
        return r.route_sem.at[2 * k], r.route_sem.at[2 * k + 1]

    def piece(place, inter):
        rows, cols = inter.shape[1:]
        across = n // (frames // rows)
        return (
            pl.ds(pl.multiple_of((place // across) * rows, rows), rows),
            pl.ds(pl.multiple_of(lax.rem(place, across) * cols, cols), cols),
        )

    def spread(source, inter, k):
        ssem, rsem = sems(k)

        def send(step):
            to = lax.rem(me_d + 1 + step, n)
            at = piece(to, inter)
            remote(source.at[at[0], at[1]], inter.at[me_d], ssem, rsem, dp=to).start()

        loop(n - 1, send)

    def spread_own(source, inter):
        at = piece(me_d, inter)
        inter[me_d] = source[at[0], at[1]]

    def settle(view, k):
        ssem, rsem = sems(k)
        view = view.at[pl.ds(0, n - 1)]
        drain(view, rsem)
        drain(view, ssem)

    def deliver(inter, stage, target, k):
        ssem, rsem = sems(k)
        at = piece(me_d, inter)

        def send(step):
            to = lax.rem(me_d + 1 + step, n)
            stage[to] = inter[r.plan[to]]
            remote(stage.at[to], target.at[at[0], at[1]], ssem, rsem, dp=to).start()

        loop(n - 1, send)
        target[at[0], at[1]] = inter[r.plan[me_d]]

    def widen(target, ssem, rsem, first_sem):
        return [
            remote(
                target.at[pl.ds(0, frames)],
                target.at[pl.ds(step * frames, frames)],
                ssem.at[first_sem + step - 1],
                rsem.at[first_sem + step - 1],
                seq=lax.rem(me_s + q - step, q),
            )
            for step in range(1, q)
        ]

    def start(copies):
        for copy in copies:
            copy.start()

    def wait(copies):
        for copy in copies:
            copy.wait()

    half_cols = width // 2
    me_block = (me_d * q + me_s) // (1 << low)
    gran = width >> len(order)

    class Sum:
        def __init__(self, group, sequences, refs):
            self.group, self.rest = group, [e for e in order if e not in group]
            self.members, self.depth = 1 << len(group), len(self.rest)
            self.plans = [schedule(self.rest, sequence, gran) for sequence in sequences]
            self.cols = width // len(sequences)
            (self.left, self.right, self.staged, self.total, self.out, self.arrived, self.swap_sem, self.sum_sem) = refs
            self.rows = self.total.shape[0]
            self.k = 0

        def swap(self, side, v):
            rows = pl.ds(v * frames, frames)
            source, target = ((self.staged.at[v - 1], self.left.at[:, rows]), (self.right.at[pl.ds(0, frames)], self.right.at[rows]))[side]
            at = 2 * v + side
            return remote(source, target, self.swap_sem.at[0, at], self.swap_sem.at[1, at], **away(self.group, v))

        def give_right(self):
            for v in range(1, self.members):
                self.swap(1, v).start()

        def give_left(self, source):
            def turn(c):
                r.turned[span(c, LANES), :] = source[:, span(c, LANES)].astype(F32).T.astype(BF16)

            loop(pairs, turn)
            for v in reversed(range(self.members)):
                for w in range(1 << self.depth):
                    block = me_block
                    flips = [e for k, e in enumerate(self.group) if (v >> k) & 1]
                    flips += [e for k, e in enumerate(self.rest) if (w >> (self.depth - 1 - k)) & 1]
                    for _, _, place in flips:
                        step = 1 << (place - low)
                        block = block + (1 - 2 * lax.rem(me_block // step, 2)) * step
                    piece_ = r.turned[pl.ds(pl.multiple_of(block * gran, gran), gran), :]
                    if v:
                        self.staged[v - 1, pl.ds(w * gran, gran), :] = piece_
                    else:
                        self.left[pl.ds(w * gran, gran), pl.ds(0, frames)] = piece_
                if v:
                    self.swap(0, v).start()

        def multiply(self):
            for v in range(1, self.members):
                self.swap(0, v).wait()
                self.swap(1, v).wait()

            def tile(i):
                self.total[:, span(i, TILE)] = dot(self.left[...], self.right[:, span(i, TILE)])

            loop(tiles, tile)
            self.start()

        def copy(self, part):
            rows = pl.ds(self.rows - (self.rows >> self.k), self.rows >> (self.k + 1))
            cols = pl.ds(part * self.cols, self.cols)
            at = part * self.depth + self.k
            return remote(
                self.out.at[rows, cols],
                self.arrived.at[rows, cols],
                self.sum_sem.at[0, at],
                self.sum_sem.at[1, at],
                **partner(self.plans[part][self.k][0]),
            )

        def start(self):
            for part, plan in enumerate(self.plans):
                at = self.rows - (self.rows >> self.k)
                cols = pl.ds(part * self.cols, self.cols)
                for row, size in plan[self.k][1]:

                    def put(i, row=row, at=at, cols=cols):
                        self.out[pl.ds(pl.multiple_of(at + i * SUB, SUB), SUB), cols] = self.total[
                            pl.ds(pl.multiple_of(row + i * SUB, SUB), SUB), cols
                        ].astype(BF16)

                    loop(size // SUB, put)
                    at += size
                self.copy(part).start()

        def finish(self):
            for part, plan in enumerate(self.plans):
                self.copy(part).wait()
                at = self.rows - (self.rows >> self.k)
                cols = pl.ds(part * self.cols, self.cols)
                for row, size in plan[self.k][2]:

                    def add(i, row=row, at=at, cols=cols):
                        rows = pl.ds(pl.multiple_of(row + i * SUB, SUB), SUB)
                        self.total[rows, cols] = self.total[rows, cols] + self.arrived[
                            pl.ds(pl.multiple_of(at + i * SUB, SUB), SUB), cols
                        ].astype(F32)

                    loop(size // SUB, add)
                    at += size
            self.k += 1

        def step(self):
            if self.k < self.depth:
                self.finish()
                if self.k < self.depth:
                    self.start()

    in_rest = list(range(len(order) - len(in_group)))
    seqs = len([e for e in order if e[0] == "seq"])
    swap_rest = [seqs] + in_rest[:seqs] + in_rest[seqs + 1 :] if seqs < len(in_rest) else in_rest
    in_sum = Sum(
        in_group,
        [in_rest, swap_rest],
        (r.in_left, r.in_right, r.in_staged, r.in_total, r.in_out, r.in_in, r.in_swap, r.in_sum),
    )
    out_sum = Sum(
        out_group,
        [list(range(len(order) - len(out_group)))],
        (r.out_left, r.out_right, r.out_staged, r.out_total, r.out_out, r.out_in, r.out_swap, r.out_sum),
    )

    inters = [r.inter_q, r.inter_k, r.inter_v]
    stages = [r.stage.at[a] for a in range(3)]
    slots = [r.slot.at[a] for a in range(3)]
    for a, source in enumerate((r.queries.at[0], r.keys.at[0], r.values.at[0])):
        spread(source, inters[a], a)

    load_g.wait()
    r.out_right[pl.ds(0, frames), :] = r.g_in[...]
    out_sum.give_right()

    def onward(a):
        settle(inters[a], a)
        deliver(inters[a], stages[a], slots[a], 3 + a)

    wide = [widen(slots[a], r.wide_send, r.wide_recv, (q - 1) * a) for a in range(3)]

    def outward(a):
        settle(stages[a], 3 + a)
        start(wide[a])

    def row_ids(row, step):
        block = lax.rem(me_s + step + q, q)
        line = r.segments[pl.ds(row, 1), :]
        chosen = line[:, :frames]
        for b in range(1, q):
            chosen = jnp.where(block == b, line[:, b * frames : (b + 1) * frames], chosen)
        return chosen.astype(F32)

    def col_ids(row, step):
        return jnp.broadcast_to(row_ids(row, step), (LANES, frames)).T

    own_col = col_ids(me_d, 0)
    for step in range(q):
        r.bias[:, pl.ds(step * frames, frames)] = jnp.where(own_col[:, :1] == row_ids(me_d, step), 0.0, MASKED)
    before = jnp.where(me_s > 0, col_ids(me_d, -1)[frames - SUB :], -1.0)
    after = jnp.where(me_s < q - 1, col_ids(me_d, 1)[:SUB], -1.0)
    r.id_pad[pl.ds(0, SUB)] = before
    r.id_pad[pl.ds(SUB, frames)] = own_col
    r.id_pad[pl.ds(SUB + frames, SUB)] = after
    for tap in range(taps):
        r.same[tap] = jnp.where(r.id_pad[pl.ds(SUB - reach + tap, frames)] == own_col, 1.0, 0.0)
    r.taps_f[pl.ds(0, taps)] = r.kernel[...].astype(F32)
    slot_pack = r.plan[me_d]
    for b in range(q):
        col = col_ids(slot_pack, b)
        for step in range(q):
            r.slot_bias[pl.ds(b * frames, frames), pl.ds(step * frames, frames)] = jnp.where(
                col[:, :1] == row_ids(slot_pack, step), 0.0, MASKED
            )

    load_po.wait()

    def act_tile(i):
        r.act_grad[:, span(i, TILE)] = dot_t(r.g_in[...], r.po[span(i, TILE), :])

    loop(tiles, act_tile)

    lane = lax.broadcasted_iota(jnp.int32, (1, LANES), 1)
    first = jnp.where(lane < HEAD_DIM, 1.0, 0.0)
    heads_low = (first.astype(BF16), (1.0 - first).astype(BF16))

    def stacked(two, factor=1.0):
        return jnp.concatenate([two * (h * factor).astype(BF16) for h in heads_low], 0)

    def merged(tall):
        return jnp.where(lane < HEAD_DIM, tall[:frames], tall[frames:])

    def softmax(scores, bias):
        scores = scores + jnp.concatenate([bias, bias], 0)
        raised = jnp.exp(scores - jnp.max(scores, -1, keepdims=True))
        return raised * (1.0 / jnp.sum(raised, -1, keepdims=True))

    load_q.wait()
    load_k.wait()
    load_v.wait()
    for a, source in enumerate((r.q_in, r.k_all, r.v_all)):
        spread_own(source, inters[a])

    def attend_part(part):
        for step in range(1, q):
            for which in range(2):
                pair_copy(which, step, part).wait()

        def attend(i):
            at = span(part * (TILE // LANES) + i, LANES)
            weights = softmax(dot_t(stacked(r.q_in[:, at], scale), r.k_all[:, at]), r.bias[...])
            r.mixed[:, at] = merged(dot(weights.astype(BF16), r.v_all[:, at])).astype(BF16)

        loop(TILE // LANES, attend)

    loop(parts - 1, attend_part)
    onward(0)
    attend_part(parts - 1)
    onward(1)

    load_x.wait()
    load_ao.wait()

    def hidden_tile(i):
        at = span(i, TILE)
        r.hat_in[:, at] = r.x_in[:, at].astype(F32) + dot(r.mixed[...], r.ao[:, at])

    loop(tiles, hidden_tile)

    def norm_rows(i):
        at = span(i, SUB)
        hidden = r.hat_in[at, :]
        shifted = hidden - jnp.mean(hidden, -1, keepdims=True)
        inverse = lax.rsqrt(jnp.mean(shifted * shifted, -1, keepdims=True) + EPSILON)
        normed = shifted * inverse
        r.hat_in[at, :] = normed
        r.inv_in[at, :] = jnp.broadcast_to(inverse, (SUB, LANES))
        r.low[at, :] = (normed * r.norm_gain[...]).astype(BF16)

    rows_loop(frames // SUB, norm_rows)
    load_pin.wait()

    def gate_tile(i):
        at = span(i, TILE)
        linear = dot(r.low[...], r.pin[:, at])
        logistic = jax.nn.sigmoid(dot(r.low[...], r.pin[:, span(i + tiles, TILE)]))
        conv_in = (linear * logistic).astype(BF16)
        r.linear[:, at] = linear
        r.logistic[:, at] = logistic
        r.conv_in[:, at] = conv_in
        wide = conv_in.astype(F32)
        for c in range(TILE // LANES):
            r.x_pad[i * (TILE // LANES) + c, pl.ds(SUB, frames), :] = wide[:, c * LANES : (c + 1) * LANES]

    loop(tiles, gate_tile)

    def edges(source, halo, at):
        return (
            remote(
                source.at[pl.ds(frames - SUB, SUB)],
                halo.at[0],
                r.edge_send.at[at],
                r.edge_recv.at[at],
                seq=lax.rem(me_s + 1, q),
            ),
            remote(
                source.at[pl.ds(0, SUB)],
                halo.at[1],
                r.edge_send.at[at + 1],
                r.edge_recv.at[at + 1],
                seq=lax.rem(me_s + q - 1, q),
            ),
        )

    def land(halo, pad):
        def put(c):
            at = span(c, LANES)
            pad[c, pl.ds(0, SUB), :] = halo[0, :, at].astype(F32)
            pad[c, pl.ds(SUB + frames, SUB), :] = halo[1, :, at].astype(F32)

        loop(pairs, put)

    edge_in = edges(r.conv_in, r.halo_in, 0)
    for copy in edge_in:
        copy.start()

    onward(2)
    in_sum.give_left(r.mixed)

    for copy in edge_in:
        copy.wait()
    land(r.halo_in, r.x_pad)

    def conv_tile(c):
        total = jnp.zeros((frames, LANES), F32)
        for tap in range(taps):
            moved = r.x_pad[c, pl.ds(SUB - reach + tap, frames), :] * r.same[tap]
            total = total + r.taps_f[tap : tap + 1, span(c, LANES)] * moved
        r.work[:, span(c, LANES)] = total

    loop(pairs, conv_tile)

    def mid_rows(i):
        at = span(i, SUB)
        conv = r.work[at, :]
        shifted = conv - jnp.mean(conv, -1, keepdims=True)
        inverse = lax.rsqrt(jnp.mean(shifted * shifted, -1, keepdims=True) + EPSILON)
        hat = shifted * inverse
        gain = r.conv_gain[...]
        normed = hat * gain
        logistic = jax.nn.sigmoid(normed)
        r.low[at, :] = (normed * logistic).astype(BF16)
        scaled = r.act_grad[at, :] * (logistic * (1.0 + normed * (1.0 - logistic))) * gain
        grad = inverse * (
            scaled - jnp.mean(scaled, -1, keepdims=True) - hat * jnp.mean(scaled * hat, -1, keepdims=True)
        )
        r.conv_grad[at, :] = grad.astype(BF16)
        for c in range(pairs):
            r.g_pad[c, pl.ds(i * SUB + SUB, SUB), :] = grad[:, c * LANES : (c + 1) * LANES]

    rows_loop(frames // SUB, mid_rows)
    edge_out = edges(r.conv_grad, r.halo_out, 2)
    for copy in edge_out:
        copy.start()

    out_sum.give_left(r.low)
    outward(0)

    for copy in edge_out:
        copy.wait()
    land(r.halo_out, r.g_pad)

    def back_tile(c):
        at = span(c, LANES)
        own = r.x_pad[c, pl.ds(SUB, frames), :]
        total = jnp.zeros((frames, LANES), F32)
        for tap in range(taps):
            moved = r.g_pad[c, pl.ds(SUB - reach + tap, frames), :] * r.same[tap]
            back = taps - 1 - tap
            total = total + r.taps_f[back : back + 1, at] * moved
            r.tap_sum[back : back + 1, at] = jnp.sum(own * moved, 0, keepdims=True)
        linear, logistic = r.linear[:, at], r.logistic[:, at]
        gated = total * logistic
        r.both_grad[:, at] = gated.astype(BF16)
        r.both_grad[:, span(c + pairs, LANES)] = (gated * linear * (1.0 - logistic)).astype(BF16)

    tap_rows = r.tap_sum.shape[0]
    r.tap_sum[pl.ds(tap_rows - SUB, SUB), :] = jnp.zeros((SUB, width), F32)
    loop(pairs, back_tile)

    everyone = bits_of(n, q)

    def tap_copy(k):
        return remote(
            r.tap_out.at[k], r.tap_in.at[k], r.tap_send.at[k], r.tap_recv.at[k], **partner(everyone[k])
        )

    def tap_start(k):
        rounded = r.tap_sum[...].astype(BF16)
        r.tap_out[k] = rounded
        tap_copy(k).start()

    def tap_finish(k):
        tap_copy(k).wait()
        r.tap_sum[...] = r.tap_out[k].astype(F32) + r.tap_in[k].astype(F32)

    tap_at = [0]

    def tap_next():
        if tap_at[0] < len(everyone):
            tap_finish(tap_at[0])
            tap_at[0] += 1
            if tap_at[0] < len(everyone):
                tap_start(tap_at[0])

    tap_start(0)
    outward(1)
    out_sum.multiply()

    def back_in_tile(i):
        r.work[:, span(i, TILE)] = dot_t(r.both_grad[...], r.pin[span(i, TILE), :])

    tap_next()
    loop(tiles, back_in_tile)

    def stream_rows(i):
        at = span(i, SUB)
        hat = r.hat_in[at, :]
        scaled = r.work[at, :] * r.norm_gain[...]
        grad = r.inv_in[at, :][:, :1] * (
            scaled - jnp.mean(scaled, -1, keepdims=True) - hat * jnp.mean(scaled * hat, -1, keepdims=True)
        )
        done = (r.g_in[at, :].astype(F32) + grad).astype(BF16)
        r.in_right[at, :] = done
        for h in range(2):
            r.stream_two[h, at, :] = done[:, h * half_cols : (h + 1) * half_cols]

    rows_loop(frames // SUB, stream_rows)
    twos = [r.stream_two.at[h] for h in range(2)]
    inters_s = [r.inter_a, r.inter_b]
    stages_s = [r.stage_s.at[h] for h in range(2)]
    slots_s = [r.slot_s.at[h] for h in range(2)]
    wide_s = [widen(slots_s[h], r.wide_send_s, r.wide_recv_s, (q - 1) * h) for h in range(2)]
    for h in range(2):
        spread(twos[h], inters_s[h], 6 + h)
    for h in range(2):
        spread_own(twos[h], inters_s[h])
    in_sum.give_right()
    tap_next()
    out_sum.step()
    in_sum.multiply()

    def pass_on(h):
        settle(inters_s[h], 6 + h)
        deliver(inters_s[h], stages_s[h], slots_s[h], 8 + h)

    def pass_wide(h):
        settle(stages_s[h], 8 + h)
        start(wide_s[h])

    def slot_weights(i, b):
        rows, at = span(b, frames), span(i, LANES)
        queries = stacked(r.slot[0, rows, at], scale)
        return softmax(dot_t(queries, r.slot[1, :, at]), r.slot_bias[rows, :])

    def weigh(first_pair, count):
        if r.kept.shape[0] < pairs:
            return

        def one(i):
            def of_block(b):
                r.kept[first_pair + i, b] = slot_weights(first_pair + i, b)

            loop(q, of_block)

        loop(count, one)

    pass_on(0)
    outward(2)
    tap_next()
    pass_on(1)
    out_sum.step()
    wait(wide[0])
    wait(wide[1])
    weigh(0, pairs // 2)
    tap_next()
    in_sum.step()
    pass_wide(0)
    weigh(pairs // 2, pairs - pairs // 2)
    pass_wide(1)
    tap_next()
    out_sum.step()
    in_sum.step()
    wait(wide[2])
    wait(wide_s[0])
    wait(wide_s[1])
    for h in range(2):
        r.stream_grad[0, :, pl.ds(h * half_cols, half_cols)] = r.slot_s[h, pl.ds(0, frames), :]

    def mixed_tile(i):
        r.mixed_grad[:, span(i, TILE)] = (
            dot_t(r.slot_s[0], r.ao[span(i, TILE), pl.ds(0, half_cols)])
            + dot_t(r.slot_s[1], r.ao[span(i, TILE), pl.ds(half_cols, half_cols)])
        ).astype(BF16)

    loop(tiles, mixed_tile)

    def back_pair(i):
        at = span(i, LANES)
        key_two, value_two = r.slot[1, :, at], r.slot[2, :, at]

        def block(b):
            rows = span(b, frames)
            queries = stacked(r.slot[0, rows, at], scale)
            grads = stacked(r.mixed_grad[rows, at])
            weights = r.kept[i, b] if r.kept.shape[0] == pairs else slot_weights(i, b)
            slope = dot_t(grads, value_two)
            delta = jnp.sum(weights * slope, -1, keepdims=True)
            score_grad = (weights * (slope - delta)).astype(BF16)
            return (
                score_grad,
                t_dot(score_grad[:, :frames], queries),
                t_dot(weights[:, :frames].astype(BF16), grads),
            )

        score_grad, key_part, value_part = block(0)
        r.query_grad[0, :, at] = (merged(dot(score_grad, key_two)) * scale).astype(BF16)

        def more(b, carry):
            _, key_more, value_more = block(b)
            return carry[0] + key_more, carry[1] + value_more

        key_part, value_part = lax.fori_loop(1, q, more, (key_part, value_part))
        r.key_grad[0, :, at] = key_part.astype(BF16)
        r.value_grad[0, :, at] = value_part.astype(BF16)

    def between(first_pair, count):
        loop(count, lambda i: back_pair(first_pair + i))

    rest = max(in_sum.depth - in_sum.k, 1)
    done = 0
    for k in range(rest):
        until = pairs * (k + 1) // rest
        between(done, until - done)
        done = until
        out_sum.step()
        in_sum.step()
    while tap_at[0] < len(everyone):
        tap_next()
    while max(in_sum.depth - in_sum.k, out_sum.depth - out_sum.k) > 0:
        out_sum.step()
        in_sum.step()
    r.kernel_grad[...] = r.tap_sum[pl.ds(0, taps), :]
    r.proj[:, pl.ds(0, width)] = r.in_total[pl.ds(0, gran), :]
    r.proj[:, pl.ds(width, width)] = r.out_total[pl.ds(0, gran), :]


def handed_out(*refs):
    count = len(refs) // 2
    for i in range(count):
        refs[count + i][...] = refs[i][...]


def swapped(cells, axis, bit):
    return lax.ppermute(cells, axis, [(i, i ^ (1 << bit)) for i in range(lax.axis_size(axis))])


def finished(cells, left, low):
    for axis, bit, place in sorted(left, key=lambda e: -e[2]):
        mine = (lax.axis_index(axis) >> bit) & 1
        split = cells.reshape(2, -1, cells.shape[1])
        out = lax.dynamic_index_in_dim(split, 1 - mine, 0, keepdims=False)
        cells = lax.dynamic_index_in_dim(split, mine, 0, keepdims=False) + swapped(
            out.astype(BF16), axis, bit
        ).astype(F32)
    return cells


def per_device(
    queries, keys, values, stream, cotangent, attn_out, point_in, kernel, point_out, norm_gain, conv_gain, segments, plan
):
    n, q = lax.axis_size("dp"), lax.axis_size("seq")
    frames, width = queries.shape[1:]
    taps = kernel.shape[0]
    whole = q * frames
    pairs = width // LANES
    rows_c, cols_c = chunking(n, frames, width)
    rows_s, cols_s = chunking(n, frames, width // 2)
    keep = pairs * q * 2 * frames * whole * 4 <= KEPT
    order, left, low = split_bits(n, q, width)
    depth = len(order)
    everyone = len(bits_of(n, q))
    parts = width // TILE
    tap_rows = -(-taps // SUB) * SUB
    any_, vmem, smem = (pl.BlockSpec(memory_space=m) for m in (pl.ANY, pltpu.VMEM, pltpu.SMEM))
    ins = dict(
        queries=any_,
        keys=any_,
        values=any_,
        stream=any_,
        cotangent=any_,
        attn_out=any_,
        point_in=any_,
        kernel=vmem,
        point_out=any_,
        norm_gain=vmem,
        conv_gain=vmem,
        segments=vmem,
        plan=smem,
    )
    low_block = jax.ShapeDtypeStruct((1, frames, width), BF16)
    outs = dict(
        query_grad=low_block,
        key_grad=low_block,
        value_grad=low_block,
        stream_grad=low_block,
        kernel_grad=jax.ShapeDtypeStruct((taps, width), F32),
        proj=jax.ShapeDtypeStruct((width >> depth, 2 * width), F32),
    )
    dma = pltpu.SemaphoreType.DMA

    def low_(*shape):
        return pltpu.VMEM(shape, BF16)

    def full_(*shape):
        return pltpu.VMEM(shape, F32)

    padded = frames + 2 * SUB
    sums = {}
    for name, group, sequences in zip(("in_", "out_"), groups_of(order), (2, 1)):
        members, rows = 1 << len(group), width >> len(group)
        made = dict(
            left=low_(rows, members * frames),
            right=low_(members * frames, width),
            staged=low_(members - 1, rows, frames),
            total=full_(rows, width),
            out=low_(rows, width),
            swap=dma((2, 2 * members)),
            sum=dma((2, sequences * (depth - len(group)))),
        )
        made.update({"in": low_(rows, width)})
        sums.update({name + key: value for key, value in made.items()})
    scratch = dict(
        g_in=low_(frames, width),
        po=low_(width, width),
        q_in=low_(frames, width),
        x_in=low_(frames, width),
        ao=low_(width, width),
        pin=low_(width, 2 * width),
        k_all=low_(whole, width),
        v_all=low_(whole, width),
        inter_q=low_(n, rows_c, cols_c),
        inter_k=low_(n, rows_c, cols_c),
        inter_v=low_(n, rows_c, cols_c),
        stage=low_(3, n, rows_c, cols_c),
        slot=low_(3, whole, width),
        inter_a=low_(n, rows_s, cols_s),
        inter_b=low_(n, rows_s, cols_s),
        stage_s=low_(2, n, rows_s, cols_s),
        slot_s=low_(2, whole, width // 2),
        kept=full_(pairs if keep else 1, q, 2 * frames, whole),
        bias=full_(frames, whole),
        slot_bias=full_(whole, whole),
        id_pad=full_(padded, LANES),
        same=full_(taps, frames, LANES),
        taps_f=full_(tap_rows, width),
        act_grad=full_(frames, width),
        mixed=low_(frames, width),
        hat_in=full_(frames, width),
        inv_in=full_(frames, LANES),
        low=low_(frames, width),
        linear=full_(frames, width),
        logistic=full_(frames, width),
        conv_in=low_(frames, width),
        conv_grad=low_(frames, width),
        x_pad=full_(pairs, padded, LANES),
        g_pad=full_(pairs, padded, LANES),
        halo_in=low_(2, SUB, width),
        halo_out=low_(2, SUB, width),
        work=full_(frames, width),
        turned=low_(width, frames),
        **sums,
        tap_sum=full_(tap_rows, width),
        tap_out=low_(everyone, tap_rows, width),
        tap_in=low_(everyone, tap_rows, width),
        both_grad=low_(frames, 2 * width),
        stream_two=low_(2, frames, width // 2),
        mixed_grad=low_(whole, width),
        load_sem=dma((8,)),
        kv_send=dma(((q - 1) * parts * 2,)),
        kv_recv=dma(((q - 1) * parts * 2,)),
        route_sem=dma((20,)),
        wide_send=dma(((q - 1) * 3,)),
        wide_recv=dma(((q - 1) * 3,)),
        wide_send_s=dma((2 * (q - 1),)),
        wide_recv_s=dma((2 * (q - 1),)),
        edge_send=dma((4,)),
        edge_recv=dma((4,)),
        tap_send=dma((everyone,)),
        tap_recv=dma((everyone,)),
    )
    names = (*ins, *outs, *scratch)
    query_grad, key_grad, value_grad, stream_grad, kernel_grad, proj = pl.pallas_call(
        functools.partial(body, n, q, names),
        out_shape=tuple(outs.values()),
        in_specs=list(ins.values()),
        out_specs=(vmem,) * len(outs),
        scratch_shapes=list(scratch.values()),
        compiler_params=pltpu.CompilerParams(
            collective_id=0, has_side_effects=True, vmem_limit_bytes=60 * 2**20
        ),
    )(
        queries,
        keys,
        values,
        stream,
        cotangent,
        attn_out,
        point_in,
        kernel,
        point_out,
        norm_gain.reshape(1, width),
        conv_gain.reshape(1, width),
        segments,
        plan,
    )
    results = (query_grad, key_grad, value_grad, stream_grad, kernel_grad, finished(proj, left, low))
    return pl.pallas_call(
        handed_out,
        out_shape=tuple(jax.ShapeDtypeStruct(x.shape, x.dtype) for x in results),
        in_specs=[vmem] * len(results),
        out_specs=(vmem,) * len(results),
    )(*results)


def solution(mesh):
    rows = P("dp", "seq", None)
    return jax.shard_map(
        per_device,
        mesh=mesh,
        in_specs=(rows,) * 5 + (P(),) * 8,
        out_specs=(rows,) * 4 + (P(), P(("dp", "seq"), None)),
        check_vma=False,
    )
```

```python
import functools
import types

import jax
import jax.numpy as jnp
from jax import lax
from jax.experimental import pallas as pl
from jax.experimental.pallas import tpu as pltpu
from jax.sharding import PartitionSpec as P

HEAD_DIM = 64
EPSILON = 1e-05
MASKED = -1e30
LANES = 128
TILE = 256
SUB = 16
KEPT = 8 * 2**20
F32 = jnp.float32
BF16 = jnp.bfloat16


def dot(left, right):
    return jnp.dot(left, right, preferred_element_type=F32)


def dot_t(left, right):
    return lax.dot_general(left, right, (((1,), (1,)), ((), ())), preferred_element_type=F32)


def t_dot(left, right):
    return lax.dot_general(left, right, (((0,), (0,)), ((), ())), preferred_element_type=F32)


def loop(count, body):
    def step(i, carry):
        body(i)
        return carry

    lax.fori_loop(0, count, step, 0)


def span(i, size):
    if isinstance(i, int):
        return pl.ds(i * size, size)
    return pl.ds(pl.multiple_of(i * size, size), size)


def rows_loop(count, body):
    for i in range(count):
        body(i)


def log2(count):
    return (count - 1).bit_length()


def chunking(count, rows, width):
    down = min(count, rows // SUB)
    return rows // down, width // (count // down)


def bits_of(n, q):
    seqs = log2(q)
    return (
        [("dp", bit, seqs + bit) for bit in range(min(1, log2(n)))]
        + [("seq", bit, bit) for bit in range(seqs)]
        + [("dp", bit, seqs + bit) for bit in range(1, log2(n))]
    )


def split_bits(n, q, width):
    low = 0
    while (width >> (log2(n) + log2(q) - low)) < SUB:
        low += 1
    order = bits_of(n, q)
    return [e for e in order if e[2] >= low], [e for e in order if e[2] < low], low


def groups_of(order):
    dps = [e for e in order if e[0] == "dp"]
    return dps[:1], dps[:1] + [e for e in order if e[0] == "seq"]


def runs_of(blocks, rows):
    runs = []
    for block in blocks:
        if runs and runs[-1][0] + runs[-1][1] == block * rows:
            runs[-1][1] += rows
        else:
            runs.append([block * rows, rows])
    return runs


def schedule(order, sequence, rows):
    depth = len(order)
    kept = list(range(1 << depth))
    plan = []
    for which in sequence:
        bit = 1 << (depth - 1 - which)
        plan.append((order[which], runs_of([u for u in kept if u & bit], rows), runs_of([u for u in kept if not u & bit], rows)))
        kept = [u for u in kept if not u & bit]
    return plan


def body(n, q, names, *refs):
    r = types.SimpleNamespace(**dict(zip(names, refs)))
    frames, width = r.x_in.shape
    whole = q * frames
    taps = r.kernel.shape[0]
    reach = taps // 2
    pairs = width // LANES
    parts = width // TILE
    tiles = width // TILE
    me_d, me_s = lax.axis_index("dp"), lax.axis_index("seq")
    scale = HEAD_DIM ** (-0.5)
    order, _, low = split_bits(n, q, width)

    def remote(src, dst, ssem, rsem, dp=None, seq=None):
        return pltpu.make_async_remote_copy(
            src_ref=src,
            dst_ref=dst,
            send_sem=ssem,
            recv_sem=rsem,
            device_id=(me_d if dp is None else dp, me_s if seq is None else seq),
            device_id_type=pl.DeviceIdType.MESH,
        )

    def drain(view, sem):
        pltpu.make_async_copy(view, view, sem).wait()

    def flipped(place, bit):
        mine = lax.rem(place // (1 << bit), 2)
        return place + (1 - 2 * mine) * (1 << bit)

    def partner(entry):
        axis, bit, _ = entry
        if axis == "dp":
            return dict(dp=flipped(me_d, bit))
        return dict(seq=flipped(me_s, bit))

    loads = [
        (r.keys.at[0], r.k_all.at[pl.ds(0, frames)]),
        (r.values.at[0], r.v_all.at[pl.ds(0, frames)]),
        (r.cotangent.at[0], r.g_in),
        (r.point_out, r.po),
        (r.queries.at[0], r.q_in),
        (r.stream.at[0], r.x_in),
        (r.attn_out, r.ao),
        (r.point_in, r.pin),
    ]
    loads = [pltpu.make_async_copy(src, dst, r.load_sem.at[at]) for at, (src, dst) in enumerate(loads)]
    for copy in loads:
        copy.start()
    load_k, load_v, load_g, load_po, load_q, load_x, load_ao, load_pin = loads

    def away(entries, v):
        place = dict(dp=me_d, seq=me_s)
        for k, (axis, bit, _) in enumerate(entries):
            if (v >> k) & 1:
                place[axis] = flipped(place[axis], bit)
        return place

    barrier = pltpu.get_barrier_semaphore()

    def greet_dp(step):
        pl.semaphore_signal(
            barrier, inc=1, device_id=(lax.rem(me_d + 1 + step, n), me_s), device_id_type=pl.DeviceIdType.MESH
        )

    def greet_seq(step):
        pl.semaphore_signal(
            barrier, inc=1, device_id=(me_d, lax.rem(me_s + 1 + step, q)), device_id_type=pl.DeviceIdType.MESH
        )

    loop(n - 1, greet_dp)
    loop(q - 1, greet_seq)
    in_group, out_group = groups_of(order)
    across = [
        v
        for v in range(1 << len(out_group))
        if len({axis for k, (axis, _, _) in enumerate(out_group) if (v >> k) & 1}) > 1
    ]
    for v in across:
        far = away(out_group, v)
        pl.semaphore_signal(barrier, inc=1, device_id=(far["dp"], far["seq"]), device_id_type=pl.DeviceIdType.MESH)
    pl.semaphore_wait(barrier, n + q - 2 + len(across))

    def pair_copy(which, step, part):
        source, target = ((r.keys, r.k_all), (r.values, r.v_all))[which]
        at = ((step - 1) * parts + part) * 2 + which
        return remote(
            source.at[0, :, span(part, TILE)],
            target.at[pl.ds(step * frames, frames), span(part, TILE)],
            r.kv_send.at[at],
            r.kv_recv.at[at],
            seq=lax.rem(me_s + q - step, q),
        )

    def send_part(part):
        for step in range(1, q):
            for which in range(2):
                pair_copy(which, step, part).start()

    loop(parts, send_part)

    def sems(k):
        return r.route_sem.at[2 * k], r.route_sem.at[2 * k + 1]

    def piece(place, inter):
        rows, cols = inter.shape[1:]
        across = n // (frames // rows)
        return (
            pl.ds(pl.multiple_of((place // across) * rows, rows), rows),
            pl.ds(pl.multiple_of(lax.rem(place, across) * cols, cols), cols),
        )

    def spread(source, inter, k):
        ssem, rsem = sems(k)

        def send(step):
            to = lax.rem(me_d + 1 + step, n)
            at = piece(to, inter)
            remote(source.at[at[0], at[1]], inter.at[me_d], ssem, rsem, dp=to).start()

        loop(n - 1, send)

    def spread_own(source, inter):
        at = piece(me_d, inter)
        inter[me_d] = source[at[0], at[1]]

    def settle(view, k):
        ssem, rsem = sems(k)
        view = view.at[pl.ds(0, n - 1)]
        drain(view, rsem)
        drain(view, ssem)

    def deliver(inter, stage, target, k):
        ssem, rsem = sems(k)
        at = piece(me_d, inter)

        def send(step):
            to = lax.rem(me_d + 1 + step, n)
            stage[to] = inter[r.plan[to]]
            remote(stage.at[to], target.at[at[0], at[1]], ssem, rsem, dp=to).start()

        loop(n - 1, send)
        target[at[0], at[1]] = inter[r.plan[me_d]]

    def widen(target, ssem, rsem, first_sem):
        return [
            remote(
                target.at[pl.ds(0, frames)],
                target.at[pl.ds(step * frames, frames)],
                ssem.at[first_sem + step - 1],
                rsem.at[first_sem + step - 1],
                seq=lax.rem(me_s + q - step, q),
            )
            for step in range(1, q)
        ]

    def start(copies):
        for copy in copies:
            copy.start()

    def wait(copies):
        for copy in copies:
            copy.wait()

    half_cols = width // 2
    me_block = (me_d * q + me_s) // (1 << low)
    gran = width >> len(order)

    class Sum:
        def __init__(self, group, sequences, refs):
            self.group, self.rest = group, [e for e in order if e not in group]
            self.members, self.depth = 1 << len(group), len(self.rest)
            self.plans = [schedule(self.rest, sequence, gran) for sequence in sequences]
            self.cols = width // len(sequences)
            (self.left, self.right, self.staged, self.total, self.out, self.arrived, self.swap_sem, self.sum_sem) = refs
            self.rows = self.total.shape[0]
            self.k = 0

        def swap(self, side, v):
            rows = pl.ds(v * frames, frames)
            source, target = ((self.staged.at[v - 1], self.left.at[:, rows]), (self.right.at[pl.ds(0, frames)], self.right.at[rows]))[side]
            at = 2 * v + side
            return remote(source, target, self.swap_sem.at[0, at], self.swap_sem.at[1, at], **away(self.group, v))

        def give_right(self):
            for v in range(1, self.members):
                self.swap(1, v).start()

        def give_left(self, source):
            def turn(c):
                r.turned[span(c, LANES), :] = source[:, span(c, LANES)].astype(F32).T.astype(BF16)

            loop(pairs, turn)
            for v in reversed(range(self.members)):
                for w in range(1 << self.depth):
                    block = me_block
                    flips = [e for k, e in enumerate(self.group) if (v >> k) & 1]
                    flips += [e for k, e in enumerate(self.rest) if (w >> (self.depth - 1 - k)) & 1]
                    for _, _, place in flips:
                        step = 1 << (place - low)
                        block = block + (1 - 2 * lax.rem(me_block // step, 2)) * step
                    piece_ = r.turned[pl.ds(pl.multiple_of(block * gran, gran), gran), :]
                    if v:
                        self.staged[v - 1, pl.ds(w * gran, gran), :] = piece_
                    else:
                        self.left[pl.ds(w * gran, gran), pl.ds(0, frames)] = piece_
                if v:
                    self.swap(0, v).start()

        def multiply(self):
            for v in range(1, self.members):
                self.swap(0, v).wait()
                self.swap(1, v).wait()

            def tile(i):
                self.total[:, span(i, TILE)] = dot(self.left[...], self.right[:, span(i, TILE)])

            loop(tiles, tile)
            self.start()

        def copy(self, part):
            rows = pl.ds(self.rows - (self.rows >> self.k), self.rows >> (self.k + 1))
            cols = pl.ds(part * self.cols, self.cols)
            at = part * self.depth + self.k
            return remote(
                self.out.at[rows, cols],
                self.arrived.at[rows, cols],
                self.sum_sem.at[0, at],
                self.sum_sem.at[1, at],
                **partner(self.plans[part][self.k][0]),
            )

        def start(self):
            for part, plan in enumerate(self.plans):
                at = self.rows - (self.rows >> self.k)
                cols = pl.ds(part * self.cols, self.cols)
                for row, size in plan[self.k][1]:

                    def put(i, row=row, at=at, cols=cols):
                        self.out[pl.ds(pl.multiple_of(at + i * SUB, SUB), SUB), cols] = self.total[
                            pl.ds(pl.multiple_of(row + i * SUB, SUB), SUB), cols
                        ].astype(BF16)

                    loop(size // SUB, put)
                    at += size
                self.copy(part).start()

        def finish(self):
            for part, plan in enumerate(self.plans):
                self.copy(part).wait()
                at = self.rows - (self.rows >> self.k)
                cols = pl.ds(part * self.cols, self.cols)
                for row, size in plan[self.k][2]:

                    def add(i, row=row, at=at, cols=cols):
                        rows = pl.ds(pl.multiple_of(row + i * SUB, SUB), SUB)
                        self.total[rows, cols] = self.total[rows, cols] + self.arrived[
                            pl.ds(pl.multiple_of(at + i * SUB, SUB), SUB), cols
                        ].astype(F32)

                    loop(size // SUB, add)
                    at += size
            self.k += 1

        def step(self):
            if self.k < self.depth:
                self.finish()
                if self.k < self.depth:
                    self.start()

    in_rest = list(range(len(order) - len(in_group)))
    seqs = len([e for e in order if e[0] == "seq"])
    swap_rest = [seqs] + in_rest[:seqs] + in_rest[seqs + 1 :] if seqs < len(in_rest) else in_rest
    in_sum = Sum(
        in_group,
        [in_rest, swap_rest],
        (r.in_left, r.in_right, r.in_staged, r.in_total, r.in_out, r.in_in, r.in_swap, r.in_sum),
    )
    out_sum = Sum(
        out_group,
        [list(range(len(order) - len(out_group)))],
        (r.out_left, r.out_right, r.out_staged, r.out_total, r.out_out, r.out_in, r.out_swap, r.out_sum),
    )

    inters = [r.inter_q, r.inter_k, r.inter_v]
    stages = [r.stage.at[a] for a in range(3)]
    slots = [r.slot.at[a] for a in range(3)]
    for a, source in enumerate((r.queries.at[0], r.keys.at[0], r.values.at[0])):
        spread(source, inters[a], a)

    load_g.wait()
    r.out_right[pl.ds(0, frames), :] = r.g_in[...]
    out_sum.give_right()

    def onward(a):
        settle(inters[a], a)
        deliver(inters[a], stages[a], slots[a], 3 + a)

    wide = [widen(slots[a], r.wide_send, r.wide_recv, (q - 1) * a) for a in range(3)]

    def outward(a):
        settle(stages[a], 3 + a)
        start(wide[a])

    def row_ids(row, step):
        block = lax.rem(me_s + step + q, q)
        line = r.segments[pl.ds(row, 1), :]
        chosen = line[:, :frames]
        for b in range(1, q):
            chosen = jnp.where(block == b, line[:, b * frames : (b + 1) * frames], chosen)
        return chosen.astype(F32)

    def col_ids(row, step):
        return jnp.broadcast_to(row_ids(row, step), (LANES, frames)).T

    own_col = col_ids(me_d, 0)
    for step in range(q):
        r.bias[:, pl.ds(step * frames, frames)] = jnp.where(own_col[:, :1] == row_ids(me_d, step), 0.0, MASKED)
    before = jnp.where(me_s > 0, col_ids(me_d, -1)[frames - SUB :], -1.0)
    after = jnp.where(me_s < q - 1, col_ids(me_d, 1)[:SUB], -1.0)
    r.id_pad[pl.ds(0, SUB)] = before
    r.id_pad[pl.ds(SUB, frames)] = own_col
    r.id_pad[pl.ds(SUB + frames, SUB)] = after
    for tap in range(taps):
        r.same[tap] = jnp.where(r.id_pad[pl.ds(SUB - reach + tap, frames)] == own_col, 1.0, 0.0)
    r.taps_f[pl.ds(0, taps)] = r.kernel[...].astype(F32)
    slot_pack = r.plan[me_d]
    for b in range(q):
        col = col_ids(slot_pack, b)
        for step in range(q):
            r.slot_bias[pl.ds(b * frames, frames), pl.ds(step * frames, frames)] = jnp.where(
                col[:, :1] == row_ids(slot_pack, step), 0.0, MASKED
            )

    load_po.wait()

    def act_tile(i):
        r.act_grad[:, span(i, TILE)] = dot_t(r.g_in[...], r.po[span(i, TILE), :])

    loop(tiles, act_tile)

    lane = lax.broadcasted_iota(jnp.int32, (1, LANES), 1)
    first = jnp.where(lane < HEAD_DIM, 1.0, 0.0)
    heads_low = (first.astype(BF16), (1.0 - first).astype(BF16))

    def stacked(two, factor=1.0):
        return jnp.concatenate([two * (h * factor).astype(BF16) for h in heads_low], 0)

    def merged(tall):
        return jnp.where(lane < HEAD_DIM, tall[:frames], tall[frames:])

    def softmax(scores, bias):
        scores = scores + jnp.concatenate([bias, bias], 0)
        raised = jnp.exp(scores - jnp.max(scores, -1, keepdims=True))
        return raised * (1.0 / jnp.sum(raised, -1, keepdims=True))

    load_pin.wait()

    def turn_in(i):
        for c in range(2 * width // TILE):
            r.pin_t[pl.ds(c * TILE, TILE), span(i, TILE)] = r.pin[span(i, TILE), pl.ds(c * TILE, TILE)].T

    loop(tiles, turn_in)
    load_q.wait()
    load_k.wait()
    load_v.wait()
    for a, source in enumerate((r.q_in, r.k_all, r.v_all)):
        spread_own(source, inters[a])

    def attend_part(part):
        for step in range(1, q):
            for which in range(2):
                pair_copy(which, step, part).wait()

        def attend(i):
            at = span(part * (TILE // LANES) + i, LANES)
            weights = softmax(dot_t(stacked(r.q_in[:, at], scale), r.k_all[:, at]), r.bias[...])
            r.mixed[:, at] = merged(dot(weights.astype(BF16), r.v_all[:, at])).astype(BF16)

        loop(TILE // LANES, attend)

    loop(parts - 1, attend_part)
    onward(0)
    attend_part(parts - 1)
    onward(1)

    load_x.wait()
    load_ao.wait()

    def hidden_tile(i):
        at = span(i, TILE)
        r.hat_in[:, at] = r.x_in[:, at].astype(F32) + dot(r.mixed[...], r.ao[:, at])

    loop(tiles, hidden_tile)

    def norm_rows(i):
        at = span(i, SUB)
        hidden = r.hat_in[at, :]
        shifted = hidden - jnp.mean(hidden, -1, keepdims=True)
        inverse = lax.rsqrt(jnp.mean(shifted * shifted, -1, keepdims=True) + EPSILON)
        normed = shifted * inverse
        r.hat_in[at, :] = normed
        r.inv_in[at, :] = jnp.broadcast_to(inverse, (SUB, LANES))
        r.low[at, :] = (normed * r.norm_gain[...]).astype(BF16)

    rows_loop(frames // SUB, norm_rows)

    def gate_tile(i):
        at = span(i, TILE)
        linear = dot(r.low[...], r.pin[:, at])
        logistic = jax.nn.sigmoid(dot(r.low[...], r.pin[:, span(i + tiles, TILE)]))
        conv_in = (linear * logistic).astype(BF16)
        r.linear[:, at] = linear
        r.logistic[:, at] = logistic
        r.conv_in[:, at] = conv_in
        wide = conv_in.astype(F32)
        for c in range(TILE // LANES):
            r.x_pad[i * (TILE // LANES) + c, pl.ds(SUB, frames), :] = wide[:, c * LANES : (c + 1) * LANES]

    loop(tiles, gate_tile)

    def edges(source, halo, at):
        return (
            remote(
                source.at[pl.ds(frames - SUB, SUB)],
                halo.at[0],
                r.edge_send.at[at],
                r.edge_recv.at[at],
                seq=lax.rem(me_s + 1, q),
            ),
            remote(
                source.at[pl.ds(0, SUB)],
                halo.at[1],
                r.edge_send.at[at + 1],
                r.edge_recv.at[at + 1],
                seq=lax.rem(me_s + q - 1, q),
            ),
        )

    def land(halo, pad):
        def put(c):
            at = span(c, LANES)
            pad[c, pl.ds(0, SUB), :] = halo[0, :, at].astype(F32)
            pad[c, pl.ds(SUB + frames, SUB), :] = halo[1, :, at].astype(F32)

        loop(pairs, put)

    edge_in = edges(r.conv_in, r.halo_in, 0)
    for copy in edge_in:
        copy.start()

    onward(2)
    in_sum.give_left(r.mixed)

    for copy in edge_in:
        copy.wait()
    land(r.halo_in, r.x_pad)

    def conv_tile(c):
        total = jnp.zeros((frames, LANES), F32)
        for tap in range(taps):
            moved = r.x_pad[c, pl.ds(SUB - reach + tap, frames), :] * r.same[tap]
            total = total + r.taps_f[tap : tap + 1, span(c, LANES)] * moved
        r.work[:, span(c, LANES)] = total

    loop(pairs, conv_tile)

    def mid_rows(i):
        at = span(i, SUB)
        conv = r.work[at, :]
        shifted = conv - jnp.mean(conv, -1, keepdims=True)
        inverse = lax.rsqrt(jnp.mean(shifted * shifted, -1, keepdims=True) + EPSILON)
        hat = shifted * inverse
        gain = r.conv_gain[...]
        normed = hat * gain
        logistic = jax.nn.sigmoid(normed)
        r.low[at, :] = (normed * logistic).astype(BF16)
        scaled = r.act_grad[at, :] * (logistic * (1.0 + normed * (1.0 - logistic))) * gain
        grad = inverse * (
            scaled - jnp.mean(scaled, -1, keepdims=True) - hat * jnp.mean(scaled * hat, -1, keepdims=True)
        )
        r.conv_grad[at, :] = grad.astype(BF16)
        for c in range(pairs):
            r.g_pad[c, pl.ds(i * SUB + SUB, SUB), :] = grad[:, c * LANES : (c + 1) * LANES]

    rows_loop(frames // SUB, mid_rows)
    edge_out = edges(r.conv_grad, r.halo_out, 2)
    for copy in edge_out:
        copy.start()

    out_sum.give_left(r.low)
    outward(0)

    for copy in edge_out:
        copy.wait()
    land(r.halo_out, r.g_pad)

    def back_tile(c):
        at = span(c, LANES)
        own = r.x_pad[c, pl.ds(SUB, frames), :]
        total = jnp.zeros((frames, LANES), F32)
        for tap in range(taps):
            moved = r.g_pad[c, pl.ds(SUB - reach + tap, frames), :] * r.same[tap]
            back = taps - 1 - tap
            total = total + r.taps_f[back : back + 1, at] * moved
            r.tap_sum[back : back + 1, at] = jnp.sum(own * moved, 0, keepdims=True)
        linear, logistic = r.linear[:, at], r.logistic[:, at]
        gated = total * logistic
        r.both_grad[:, at] = gated.astype(BF16)
        r.both_grad[:, span(c + pairs, LANES)] = (gated * linear * (1.0 - logistic)).astype(BF16)

    tap_rows = r.tap_sum.shape[0]
    r.tap_sum[pl.ds(tap_rows - SUB, SUB), :] = jnp.zeros((SUB, width), F32)
    loop(pairs, back_tile)

    everyone = bits_of(n, q)

    def tap_copy(k):
        return remote(
            r.tap_out.at[k], r.tap_in.at[k], r.tap_send.at[k], r.tap_recv.at[k], **partner(everyone[k])
        )

    def tap_start(k):
        rounded = r.tap_sum[...].astype(BF16)
        r.tap_out[k] = rounded
        tap_copy(k).start()

    def tap_finish(k):
        tap_copy(k).wait()
        r.tap_sum[...] = r.tap_out[k].astype(F32) + r.tap_in[k].astype(F32)

    tap_at = [0]

    def tap_next():
        if tap_at[0] < len(everyone):
            tap_finish(tap_at[0])
            tap_at[0] += 1
            if tap_at[0] < len(everyone):
                tap_start(tap_at[0])

    tap_start(0)
    outward(1)
    out_sum.multiply()

    def back_in_tile(i):
        r.work[:, span(i, TILE)] = dot(r.both_grad[...], r.pin_t[:, span(i, TILE)])

    tap_next()
    loop(tiles, back_in_tile)

    def stream_rows(i):
        at = span(i, SUB)
        hat = r.hat_in[at, :]
        scaled = r.work[at, :] * r.norm_gain[...]
        grad = r.inv_in[at, :][:, :1] * (
            scaled - jnp.mean(scaled, -1, keepdims=True) - hat * jnp.mean(scaled * hat, -1, keepdims=True)
        )
        done = (r.g_in[at, :].astype(F32) + grad).astype(BF16)
        r.in_right[at, :] = done
        for h in range(2):
            r.stream_two[h, at, :] = done[:, h * half_cols : (h + 1) * half_cols]

    rows_loop(frames // SUB, stream_rows)
    twos = [r.stream_two.at[h] for h in range(2)]
    inters_s = [r.inter_a, r.inter_b]
    stages_s = [r.stage_s.at[h] for h in range(2)]
    slots_s = [r.slot_s.at[h] for h in range(2)]
    wide_s = [widen(slots_s[h], r.wide_send_s, r.wide_recv_s, (q - 1) * h) for h in range(2)]
    for h in range(2):
        spread(twos[h], inters_s[h], 6 + h)
    for h in range(2):
        spread_own(twos[h], inters_s[h])
    in_sum.give_right()
    tap_next()
    out_sum.step()
    in_sum.multiply()

    def pass_on(h):
        settle(inters_s[h], 6 + h)
        deliver(inters_s[h], stages_s[h], slots_s[h], 8 + h)

    def pass_wide(h):
        settle(stages_s[h], 8 + h)
        start(wide_s[h])

    def slot_weights(i, b):
        rows, at = span(b, frames), span(i, LANES)
        queries = stacked(r.slot[0, rows, at], scale)
        return softmax(dot_t(queries, r.slot[1, :, at]), r.slot_bias[rows, :])

    def weigh(first_pair, count):
        if r.kept.shape[0] < pairs:
            return

        def one(i):
            def of_block(b):
                r.kept[first_pair + i, b] = slot_weights(first_pair + i, b)

            loop(q, of_block)

        loop(count, one)

    pass_on(0)
    outward(2)
    tap_next()
    pass_on(1)
    wait(wide[0])
    wait(wide[1])
    weigh(0, pairs // 2)
    in_sum.step()
    pass_wide(0)
    out_sum.step()
    tap_next()
    weigh(pairs // 2, pairs - pairs // 2)
    pass_wide(1)
    tap_next()
    in_sum.step()
    out_sum.step()
    wait(wide[2])
    wait(wide_s[0])
    wait(wide_s[1])
    for h in range(2):
        r.stream_grad[0, :, pl.ds(h * half_cols, half_cols)] = r.slot_s[h, pl.ds(0, frames), :]

    def mixed_tile(i):
        r.mixed_grad[:, span(i, TILE)] = (
            dot_t(r.slot_s[0], r.ao[span(i, TILE), pl.ds(0, half_cols)])
            + dot_t(r.slot_s[1], r.ao[span(i, TILE), pl.ds(half_cols, half_cols)])
        ).astype(BF16)

    loop(tiles, mixed_tile)

    def back_pair(i):
        at = span(i, LANES)
        key_two, value_two = r.slot[1, :, at], r.slot[2, :, at]

        def block(b):
            rows = span(b, frames)
            queries = stacked(r.slot[0, rows, at], scale)
            grads = stacked(r.mixed_grad[rows, at])
            weights = r.kept[i, b] if r.kept.shape[0] == pairs else slot_weights(i, b)
            slope = dot_t(grads, value_two)
            delta = jnp.sum(weights * slope, -1, keepdims=True)
            score_grad = (weights * (slope - delta)).astype(BF16)
            return (
                score_grad,
                t_dot(score_grad[:, :frames], queries),
                t_dot(weights[:, :frames].astype(BF16), grads),
            )

        score_grad, key_part, value_part = block(0)
        r.query_grad[0, :, at] = (merged(dot(score_grad, key_two)) * scale).astype(BF16)

        def more(b, carry):
            _, key_more, value_more = block(b)
            return carry[0] + key_more, carry[1] + value_more

        key_part, value_part = lax.fori_loop(1, q, more, (key_part, value_part))
        r.key_grad[0, :, at] = key_part.astype(BF16)
        r.value_grad[0, :, at] = value_part.astype(BF16)

    def between(first_pair, count):
        loop(count, lambda i: back_pair(first_pair + i))

    rest = max(in_sum.depth - in_sum.k, 1)
    done = 0
    for k in range(rest):
        until = pairs * (k + 1) // rest
        between(done, until - done)
        done = until
        out_sum.step()
        in_sum.step()
    while tap_at[0] < len(everyone):
        tap_next()
    while max(in_sum.depth - in_sum.k, out_sum.depth - out_sum.k) > 0:
        out_sum.step()
        in_sum.step()
    r.kernel_grad[...] = r.tap_sum[pl.ds(0, taps), :]
    r.proj[:, pl.ds(0, width)] = r.in_total[pl.ds(0, gran), :]
    r.proj[:, pl.ds(width, width)] = r.out_total[pl.ds(0, gran), :]


def handed_out(*refs):
    count = len(refs) // 2
    for i in range(count):
        refs[count + i][...] = refs[i][...]


def swapped(cells, axis, bit):
    return lax.ppermute(cells, axis, [(i, i ^ (1 << bit)) for i in range(lax.axis_size(axis))])


def finished(cells, left, low):
    for axis, bit, place in sorted(left, key=lambda e: -e[2]):
        mine = (lax.axis_index(axis) >> bit) & 1
        split = cells.reshape(2, -1, cells.shape[1])
        out = lax.dynamic_index_in_dim(split, 1 - mine, 0, keepdims=False)
        cells = lax.dynamic_index_in_dim(split, mine, 0, keepdims=False) + swapped(
            out.astype(BF16), axis, bit
        ).astype(F32)
    return cells


def per_device(
    queries, keys, values, stream, cotangent, attn_out, point_in, kernel, point_out, norm_gain, conv_gain, segments, plan
):
    n, q = lax.axis_size("dp"), lax.axis_size("seq")
    frames, width = queries.shape[1:]
    taps = kernel.shape[0]
    whole = q * frames
    pairs = width // LANES
    rows_c, cols_c = chunking(n, frames, width)
    rows_s, cols_s = chunking(n, frames, width // 2)
    keep = pairs * q * 2 * frames * whole * 4 <= KEPT
    order, left, low = split_bits(n, q, width)
    depth = len(order)
    everyone = len(bits_of(n, q))
    parts = width // TILE
    tap_rows = -(-taps // SUB) * SUB
    any_, vmem, smem = (pl.BlockSpec(memory_space=m) for m in (pl.ANY, pltpu.VMEM, pltpu.SMEM))
    ins = dict(
        queries=any_,
        keys=any_,
        values=any_,
        stream=any_,
        cotangent=any_,
        attn_out=any_,
        point_in=any_,
        kernel=vmem,
        point_out=any_,
        norm_gain=vmem,
        conv_gain=vmem,
        segments=vmem,
        plan=smem,
    )
    low_block = jax.ShapeDtypeStruct((1, frames, width), BF16)
    outs = dict(
        query_grad=low_block,
        key_grad=low_block,
        value_grad=low_block,
        stream_grad=low_block,
        kernel_grad=jax.ShapeDtypeStruct((taps, width), F32),
        proj=jax.ShapeDtypeStruct((width >> depth, 2 * width), F32),
    )
    dma = pltpu.SemaphoreType.DMA

    def low_(*shape):
        return pltpu.VMEM(shape, BF16)

    def full_(*shape):
        return pltpu.VMEM(shape, F32)

    padded = frames + 2 * SUB
    sums = {}
    for name, group, sequences in zip(("in_", "out_"), groups_of(order), (2, 1)):
        members, rows = 1 << len(group), width >> len(group)
        made = dict(
            left=low_(rows, members * frames),
            right=low_(members * frames, width),
            staged=low_(members - 1, rows, frames),
            total=full_(rows, width),
            out=low_(rows, width),
            swap=dma((2, 2 * members)),
            sum=dma((2, sequences * (depth - len(group)))),
        )
        made.update({"in": low_(rows, width)})
        sums.update({name + key: value for key, value in made.items()})
    scratch = dict(
        g_in=low_(frames, width),
        po=low_(width, width),
        q_in=low_(frames, width),
        x_in=low_(frames, width),
        ao=low_(width, width),
        pin=low_(width, 2 * width),
        pin_t=low_(2 * width, width),
        k_all=low_(whole, width),
        v_all=low_(whole, width),
        inter_q=low_(n, rows_c, cols_c),
        inter_k=low_(n, rows_c, cols_c),
        inter_v=low_(n, rows_c, cols_c),
        stage=low_(3, n, rows_c, cols_c),
        slot=low_(3, whole, width),
        inter_a=low_(n, rows_s, cols_s),
        inter_b=low_(n, rows_s, cols_s),
        stage_s=low_(2, n, rows_s, cols_s),
        slot_s=low_(2, whole, width // 2),
        kept=full_(pairs if keep else 1, q, 2 * frames, whole),
        bias=full_(frames, whole),
        slot_bias=full_(whole, whole),
        id_pad=full_(padded, LANES),
        same=full_(taps, frames, LANES),
        taps_f=full_(tap_rows, width),
        act_grad=full_(frames, width),
        mixed=low_(frames, width),
        hat_in=full_(frames, width),
        inv_in=full_(frames, LANES),
        low=low_(frames, width),
        linear=full_(frames, width),
        logistic=full_(frames, width),
        conv_in=low_(frames, width),
        conv_grad=low_(frames, width),
        x_pad=full_(pairs, padded, LANES),
        g_pad=full_(pairs, padded, LANES),
        halo_in=low_(2, SUB, width),
        halo_out=low_(2, SUB, width),
        work=full_(frames, width),
        turned=low_(width, frames),
        **sums,
        tap_sum=full_(tap_rows, width),
        tap_out=low_(everyone, tap_rows, width),
        tap_in=low_(everyone, tap_rows, width),
        both_grad=low_(frames, 2 * width),
        stream_two=low_(2, frames, width // 2),
        mixed_grad=low_(whole, width),
        load_sem=dma((8,)),
        kv_send=dma(((q - 1) * parts * 2,)),
        kv_recv=dma(((q - 1) * parts * 2,)),
        route_sem=dma((20,)),
        wide_send=dma(((q - 1) * 3,)),
        wide_recv=dma(((q - 1) * 3,)),
        wide_send_s=dma((2 * (q - 1),)),
        wide_recv_s=dma((2 * (q - 1),)),
        edge_send=dma((4,)),
        edge_recv=dma((4,)),
        tap_send=dma((everyone,)),
        tap_recv=dma((everyone,)),
    )
    names = (*ins, *outs, *scratch)
    query_grad, key_grad, value_grad, stream_grad, kernel_grad, proj = pl.pallas_call(
        functools.partial(body, n, q, names),
        out_shape=tuple(outs.values()),
        in_specs=list(ins.values()),
        out_specs=(vmem,) * len(outs),
        scratch_shapes=list(scratch.values()),
        compiler_params=pltpu.CompilerParams(
            collective_id=0, has_side_effects=True, vmem_limit_bytes=60 * 2**20
        ),
    )(
        queries,
        keys,
        values,
        stream,
        cotangent,
        attn_out,
        point_in,
        kernel,
        point_out,
        norm_gain.reshape(1, width),
        conv_gain.reshape(1, width),
        segments,
        plan,
    )
    results = (query_grad, key_grad, value_grad, stream_grad, kernel_grad, finished(proj, left, low))
    return pl.pallas_call(
        handed_out,
        out_shape=tuple(jax.ShapeDtypeStruct(x.shape, x.dtype) for x in results),
        in_specs=[vmem] * len(results),
        out_specs=(vmem,) * len(results),
    )(*results)


def solution(mesh):
    rows = P("dp", "seq", None)
    return jax.shard_map(
        per_device,
        mesh=mesh,
        in_specs=(rows,) * 5 + (P(),) * 8,
        out_specs=(rows,) * 4 + (P(), P(("dp", "seq"), None)),
        check_vma=False,
    )
```

```python
import functools
import types

import jax
import jax.numpy as jnp
from jax import lax
from jax.experimental import pallas as pl
from jax.experimental.pallas import tpu as pltpu
from jax.sharding import PartitionSpec as P

HEAD_DIM = 64
EPSILON = 1e-05
MASKED = -1e30
LANES = 128
TILE = 256
SUB = 16
KEPT = 8 * 2**20
F32 = jnp.float32
BF16 = jnp.bfloat16


def dot(left, right):
    return jnp.dot(left, right, preferred_element_type=F32)


def dot_t(left, right):
    return lax.dot_general(left, right, (((1,), (1,)), ((), ())), preferred_element_type=F32)


def t_dot(left, right):
    return lax.dot_general(left, right, (((0,), (0,)), ((), ())), preferred_element_type=F32)


def loop(count, body):
    def step(i, carry):
        body(i)
        return carry

    lax.fori_loop(0, count, step, 0)


def span(i, size):
    if isinstance(i, int):
        return pl.ds(i * size, size)
    return pl.ds(pl.multiple_of(i * size, size), size)


def rows_loop(count, body):
    for i in range(count):
        body(i)


def log2(count):
    return (count - 1).bit_length()


def chunking(count, rows, width):
    down = min(count, rows // SUB)
    return rows // down, width // (count // down)


def bits_of(n, q):
    seqs = log2(q)
    return (
        [("dp", bit, seqs + bit) for bit in range(min(1, log2(n)))]
        + [("seq", bit, bit) for bit in range(seqs)]
        + [("dp", bit, seqs + bit) for bit in range(1, log2(n))]
    )


def split_bits(n, q, width):
    low = 0
    while (width >> (log2(n) + log2(q) - low)) < SUB:
        low += 1
    order = bits_of(n, q)
    return [e for e in order if e[2] >= low], [e for e in order if e[2] < low], low


def groups_of(order):
    dps = [e for e in order if e[0] == "dp"]
    return dps[:1], dps[:1] + [e for e in order if e[0] == "seq"]


def runs_of(blocks, rows):
    runs = []
    for block in blocks:
        if runs and runs[-1][0] + runs[-1][1] == block * rows:
            runs[-1][1] += rows
        else:
            runs.append([block * rows, rows])
    return runs


def schedule(order, sequence, rows):
    depth = len(order)
    kept = list(range(1 << depth))
    plan = []
    for which in sequence:
        bit = 1 << (depth - 1 - which)
        plan.append((order[which], runs_of([u for u in kept if u & bit], rows), runs_of([u for u in kept if not u & bit], rows)))
        kept = [u for u in kept if not u & bit]
    return plan


def body(n, q, names, *refs):
    r = types.SimpleNamespace(**dict(zip(names, refs)))
    frames, width = r.x_in.shape
    whole = q * frames
    taps = r.kernel.shape[0]
    reach = taps // 2
    pairs = width // LANES
    parts = width // TILE
    tiles = width // TILE
    me_d, me_s = lax.axis_index("dp"), lax.axis_index("seq")
    scale = HEAD_DIM ** (-0.5)
    order, _, low = split_bits(n, q, width)

    def remote(src, dst, ssem, rsem, dp=None, seq=None):
        return pltpu.make_async_remote_copy(
            src_ref=src,
            dst_ref=dst,
            send_sem=ssem,
            recv_sem=rsem,
            device_id=(me_d if dp is None else dp, me_s if seq is None else seq),
            device_id_type=pl.DeviceIdType.MESH,
        )

    def drain(view, sem):
        pltpu.make_async_copy(view, view, sem).wait()

    def flipped(place, bit):
        mine = lax.rem(place // (1 << bit), 2)
        return place + (1 - 2 * mine) * (1 << bit)

    def partner(entry):
        axis, bit, _ = entry
        if axis == "dp":
            return dict(dp=flipped(me_d, bit))
        return dict(seq=flipped(me_s, bit))

    loads = [
        (r.keys.at[0], r.k_all.at[pl.ds(0, frames)]),
        (r.values.at[0], r.v_all.at[pl.ds(0, frames)]),
        (r.cotangent.at[0], r.g_in),
        (r.point_out, r.po),
        (r.queries.at[0], r.q_in),
        (r.stream.at[0], r.x_in),
        (r.attn_out, r.ao),
        (r.point_in, r.pin),
    ]
    loads = [pltpu.make_async_copy(src, dst, r.load_sem.at[at]) for at, (src, dst) in enumerate(loads)]
    for copy in loads:
        copy.start()
    load_k, load_v, load_g, load_po, load_q, load_x, load_ao, load_pin = loads

    def away(entries, v):
        place = dict(dp=me_d, seq=me_s)
        for k, (axis, bit, _) in enumerate(entries):
            if (v >> k) & 1:
                place[axis] = flipped(place[axis], bit)
        return place

    barrier = pltpu.get_barrier_semaphore()

    def greet_dp(step):
        pl.semaphore_signal(
            barrier, inc=1, device_id=(lax.rem(me_d + 1 + step, n), me_s), device_id_type=pl.DeviceIdType.MESH
        )

    def greet_seq(step):
        pl.semaphore_signal(
            barrier, inc=1, device_id=(me_d, lax.rem(me_s + 1 + step, q)), device_id_type=pl.DeviceIdType.MESH
        )

    loop(n - 1, greet_dp)
    loop(q - 1, greet_seq)
    in_group, out_group = groups_of(order)
    across = [
        v
        for v in range(1 << len(out_group))
        if len({axis for k, (axis, _, _) in enumerate(out_group) if (v >> k) & 1}) > 1
    ]
    for v in across:
        far = away(out_group, v)
        pl.semaphore_signal(barrier, inc=1, device_id=(far["dp"], far["seq"]), device_id_type=pl.DeviceIdType.MESH)
    pl.semaphore_wait(barrier, n + q - 2 + len(across))

    def pair_copy(which, step, part):
        source, target = ((r.keys, r.k_all), (r.values, r.v_all))[which]
        at = ((step - 1) * parts + part) * 2 + which
        return remote(
            source.at[0, :, span(part, TILE)],
            target.at[pl.ds(step * frames, frames), span(part, TILE)],
            r.kv_send.at[at],
            r.kv_recv.at[at],
            seq=lax.rem(me_s + q - step, q),
        )

    def send_part(part):
        for step in range(1, q):
            for which in range(2):
                pair_copy(which, step, part).start()

    loop(parts, send_part)

    def sems(k):
        return r.route_sem.at[2 * k], r.route_sem.at[2 * k + 1]

    def piece(place, inter):
        rows, cols = inter.shape[1:]
        across = n // (frames // rows)
        return (
            pl.ds(pl.multiple_of((place // across) * rows, rows), rows),
            pl.ds(pl.multiple_of(lax.rem(place, across) * cols, cols), cols),
        )

    def spread(source, inter, k):
        ssem, rsem = sems(k)

        def send(step):
            to = lax.rem(me_d + 1 + step, n)
            at = piece(to, inter)
            remote(source.at[at[0], at[1]], inter.at[me_d], ssem, rsem, dp=to).start()

        loop(n - 1, send)

    def spread_own(source, inter):
        at = piece(me_d, inter)
        inter[me_d] = source[at[0], at[1]]

    def settle(view, k):
        ssem, rsem = sems(k)
        view = view.at[pl.ds(0, n - 1)]
        drain(view, rsem)
        drain(view, ssem)

    def deliver(inter, stage, target, k):
        ssem, rsem = sems(k)
        at = piece(me_d, inter)

        def send(step):
            to = lax.rem(me_d + 1 + step, n)
            stage[to] = inter[r.plan[to]]
            remote(stage.at[to], target.at[at[0], at[1]], ssem, rsem, dp=to).start()

        loop(n - 1, send)
        target[at[0], at[1]] = inter[r.plan[me_d]]

    def widen(target, ssem, rsem, first_sem):
        return [
            remote(
                target.at[pl.ds(0, frames)],
                target.at[pl.ds(step * frames, frames)],
                ssem.at[first_sem + step - 1],
                rsem.at[first_sem + step - 1],
                seq=lax.rem(me_s + q - step, q),
            )
            for step in range(1, q)
        ]

    def start(copies):
        for copy in copies:
            copy.start()

    def wait(copies):
        for copy in copies:
            copy.wait()

    half_cols = width // 2
    me_block = (me_d * q + me_s) // (1 << low)
    gran = width >> len(order)

    class Sum:
        def __init__(self, group, sequences, refs):
            self.group, self.rest = group, [e for e in order if e not in group]
            self.members, self.depth = 1 << len(group), len(self.rest)
            self.plans = [schedule(self.rest, sequence, gran) for sequence in sequences]
            self.cols = width // len(sequences)
            (self.left, self.right, self.staged, self.total, self.out, self.arrived, self.swap_sem, self.sum_sem) = refs
            self.rows = self.total.shape[0]
            self.k = 0

        def swap(self, side, v):
            rows = pl.ds(v * frames, frames)
            source, target = ((self.staged.at[v - 1], self.left.at[:, rows]), (self.right.at[pl.ds(0, frames)], self.right.at[rows]))[side]
            at = 2 * v + side
            return remote(source, target, self.swap_sem.at[0, at], self.swap_sem.at[1, at], **away(self.group, v))

        def give_right(self):
            for v in range(1, self.members):
                self.swap(1, v).start()

        def give_left(self, source):
            def turn(c):
                r.turned[span(c, LANES), :] = source[:, span(c, LANES)].astype(F32).T.astype(BF16)

            loop(pairs, turn)
            for v in reversed(range(self.members)):
                for w in range(1 << self.depth):
                    block = me_block
                    flips = [e for k, e in enumerate(self.group) if (v >> k) & 1]
                    flips += [e for k, e in enumerate(self.rest) if (w >> (self.depth - 1 - k)) & 1]
                    for _, _, place in flips:
                        step = 1 << (place - low)
                        block = block + (1 - 2 * lax.rem(me_block // step, 2)) * step
                    piece_ = r.turned[pl.ds(pl.multiple_of(block * gran, gran), gran), :]
                    if v:
                        self.staged[v - 1, pl.ds(w * gran, gran), :] = piece_
                    else:
                        self.left[pl.ds(w * gran, gran), pl.ds(0, frames)] = piece_
                if v:
                    self.swap(0, v).start()

        def multiply(self):
            for v in range(1, self.members):
                self.swap(0, v).wait()
                self.swap(1, v).wait()

            def tile(i):
                self.total[:, span(i, TILE)] = dot(self.left[...], self.right[:, span(i, TILE)])

            loop(tiles, tile)
            self.start()

        def copy(self, part):
            rows = pl.ds(self.rows - (self.rows >> self.k), self.rows >> (self.k + 1))
            cols = pl.ds(part * self.cols, self.cols)
            at = part * self.depth + self.k
            return remote(
                self.out.at[rows, cols],
                self.arrived.at[rows, cols],
                self.sum_sem.at[0, at],
                self.sum_sem.at[1, at],
                **partner(self.plans[part][self.k][0]),
            )

        def start(self):
            for part, plan in enumerate(self.plans):
                at = self.rows - (self.rows >> self.k)
                cols = pl.ds(part * self.cols, self.cols)
                for row, size in plan[self.k][1]:

                    def put(i, row=row, at=at, cols=cols):
                        self.out[pl.ds(pl.multiple_of(at + i * SUB, SUB), SUB), cols] = self.total[
                            pl.ds(pl.multiple_of(row + i * SUB, SUB), SUB), cols
                        ].astype(BF16)

                    loop(size // SUB, put)
                    at += size
                self.copy(part).start()

        def finish(self):
            for part, plan in enumerate(self.plans):
                self.copy(part).wait()
                at = self.rows - (self.rows >> self.k)
                cols = pl.ds(part * self.cols, self.cols)
                for row, size in plan[self.k][2]:

                    def add(i, row=row, at=at, cols=cols):
                        rows = pl.ds(pl.multiple_of(row + i * SUB, SUB), SUB)
                        self.total[rows, cols] = self.total[rows, cols] + self.arrived[
                            pl.ds(pl.multiple_of(at + i * SUB, SUB), SUB), cols
                        ].astype(F32)

                    loop(size // SUB, add)
                    at += size
            self.k += 1

        def step(self):
            if self.k < self.depth:
                self.finish()
                if self.k < self.depth:
                    self.start()

    in_rest = list(range(len(order) - len(in_group)))
    seqs = len([e for e in order if e[0] == "seq"])
    swap_rest = [seqs] + in_rest[:seqs] + in_rest[seqs + 1 :] if seqs < len(in_rest) else in_rest
    in_sum = Sum(
        in_group,
        [in_rest, swap_rest],
        (r.in_left, r.in_right, r.in_staged, r.in_total, r.in_out, r.in_in, r.in_swap, r.in_sum),
    )
    out_sum = Sum(
        out_group,
        [list(range(len(order) - len(out_group)))],
        (r.out_left, r.out_right, r.out_staged, r.out_total, r.out_out, r.out_in, r.out_swap, r.out_sum),
    )

    inters = [r.inter_q, r.inter_k, r.inter_v]
    stages = [r.stage.at[a] for a in range(3)]
    slots = [r.slot.at[a] for a in range(3)]
    for a, source in enumerate((r.queries.at[0], r.keys.at[0], r.values.at[0])):
        spread(source, inters[a], a)

    load_g.wait()
    r.out_right[pl.ds(0, frames), :] = r.g_in[...]
    out_sum.give_right()

    def onward(a):
        settle(inters[a], a)
        deliver(inters[a], stages[a], slots[a], 3 + a)

    wide = [widen(slots[a], r.wide_send, r.wide_recv, (q - 1) * a) for a in range(3)]

    def outward(a):
        settle(stages[a], 3 + a)
        start(wide[a])

    def row_ids(row, step):
        block = lax.rem(me_s + step + q, q)
        line = r.segments[pl.ds(row, 1), :]
        chosen = line[:, :frames]
        for b in range(1, q):
            chosen = jnp.where(block == b, line[:, b * frames : (b + 1) * frames], chosen)
        return chosen.astype(F32)

    def col_ids(row, step):
        return jnp.broadcast_to(row_ids(row, step), (LANES, frames)).T

    own_col = col_ids(me_d, 0)
    for step in range(q):
        r.bias[:, pl.ds(step * frames, frames)] = jnp.where(own_col[:, :1] == row_ids(me_d, step), 0.0, MASKED)
    before = jnp.where(me_s > 0, col_ids(me_d, -1)[frames - SUB :], -1.0)
    after = jnp.where(me_s < q - 1, col_ids(me_d, 1)[:SUB], -1.0)
    r.id_pad[pl.ds(0, SUB)] = before
    r.id_pad[pl.ds(SUB, frames)] = own_col
    r.id_pad[pl.ds(SUB + frames, SUB)] = after
    for tap in range(taps):
        r.same[tap] = jnp.where(r.id_pad[pl.ds(SUB - reach + tap, frames)] == own_col, 1.0, 0.0)
    r.taps_f[pl.ds(0, taps)] = r.kernel[...].astype(F32)
    slot_pack = r.plan[me_d]
    for b in range(q):
        col = col_ids(slot_pack, b)
        for step in range(q):
            r.slot_bias[pl.ds(b * frames, frames), pl.ds(step * frames, frames)] = jnp.where(
                col[:, :1] == row_ids(slot_pack, step), 0.0, MASKED
            )

    load_po.wait()

    def act_tile(i):
        r.act_grad[:, span(i, TILE)] = dot_t(r.g_in[...], r.po[span(i, TILE), :])

    loop(tiles, act_tile)

    lane = lax.broadcasted_iota(jnp.int32, (1, LANES), 1)
    first = jnp.where(lane < HEAD_DIM, 1.0, 0.0)
    heads_low = (first.astype(BF16), (1.0 - first).astype(BF16))

    def stacked(two, factor=1.0):
        return jnp.concatenate([two * (h * factor).astype(BF16) for h in heads_low], 0)

    def merged(tall):
        return jnp.where(lane < HEAD_DIM, tall[:frames], tall[frames:])

    def softmax(scores, bias):
        scores = scores + jnp.concatenate([bias, bias], 0)
        raised = jnp.exp(scores - jnp.max(scores, -1, keepdims=True))
        return raised * (1.0 / jnp.sum(raised, -1, keepdims=True))

    load_q.wait()
    load_k.wait()
    load_v.wait()
    for a, source in enumerate((r.q_in, r.k_all, r.v_all)):
        spread_own(source, inters[a])

    def attend_part(part):
        for step in range(1, q):
            for which in range(2):
                pair_copy(which, step, part).wait()

        def attend(i):
            at = span(part * (TILE // LANES) + i, LANES)
            weights = softmax(dot_t(stacked(r.q_in[:, at], scale), r.k_all[:, at]), r.bias[...])
            r.mixed[:, at] = merged(dot(weights.astype(BF16), r.v_all[:, at])).astype(BF16)

        loop(TILE // LANES, attend)

    loop(parts - 1, attend_part)
    onward(0)
    attend_part(parts - 1)
    onward(1)

    load_x.wait()
    load_ao.wait()

    def hidden_tile(i):
        at = span(i, TILE)
        r.hat_in[:, at] = r.x_in[:, at].astype(F32) + dot(r.mixed[...], r.ao[:, at])

    loop(tiles, hidden_tile)

    def norm_rows(i):
        at = span(i, SUB)
        hidden = r.hat_in[at, :]
        shifted = hidden - jnp.mean(hidden, -1, keepdims=True)
        inverse = lax.rsqrt(jnp.mean(shifted * shifted, -1, keepdims=True) + EPSILON)
        normed = shifted * inverse
        r.hat_in[at, :] = normed
        r.inv_in[at, :] = jnp.broadcast_to(inverse, (SUB, LANES))
        r.low[at, :] = (normed * r.norm_gain[...]).astype(BF16)

    rows_loop(frames // SUB, norm_rows)
    load_pin.wait()

    def gate_tile(i):
        at = span(i, TILE)
        linear = dot(r.low[...], r.pin[:, at])
        logistic = jax.nn.sigmoid(dot(r.low[...], r.pin[:, span(i + tiles, TILE)]))
        conv_in = (linear * logistic).astype(BF16)
        r.linear[:, at] = linear
        r.logistic[:, at] = logistic
        r.conv_in[:, at] = conv_in
        wide = conv_in.astype(F32)
        for c in range(TILE // LANES):
            r.x_pad[i * (TILE // LANES) + c, pl.ds(SUB, frames), :] = wide[:, c * LANES : (c + 1) * LANES]

    loop(tiles, gate_tile)

    def edges(source, halo, at):
        return (
            remote(
                source.at[pl.ds(frames - SUB, SUB)],
                halo.at[0],
                r.edge_send.at[at],
                r.edge_recv.at[at],
                seq=lax.rem(me_s + 1, q),
            ),
            remote(
                source.at[pl.ds(0, SUB)],
                halo.at[1],
                r.edge_send.at[at + 1],
                r.edge_recv.at[at + 1],
                seq=lax.rem(me_s + q - 1, q),
            ),
        )

    def land(halo, pad):
        def put(c):
            at = span(c, LANES)
            pad[c, pl.ds(0, SUB), :] = halo[0, :, at].astype(F32)
            pad[c, pl.ds(SUB + frames, SUB), :] = halo[1, :, at].astype(F32)

        loop(pairs, put)

    edge_in = edges(r.conv_in, r.halo_in, 0)
    for copy in edge_in:
        copy.start()

    onward(2)
    in_sum.give_left(r.mixed)

    for copy in edge_in:
        copy.wait()
    land(r.halo_in, r.x_pad)

    def conv_tile(c):
        total = jnp.zeros((frames, LANES), F32)
        for tap in range(taps):
            moved = r.x_pad[c, pl.ds(SUB - reach + tap, frames), :] * r.same[tap]
            total = total + r.taps_f[tap : tap + 1, span(c, LANES)] * moved
        r.work[:, span(c, LANES)] = total

    loop(pairs, conv_tile)

    def mid_rows(i):
        at = span(i, SUB)
        conv = r.work[at, :]
        shifted = conv - jnp.mean(conv, -1, keepdims=True)
        inverse = lax.rsqrt(jnp.mean(shifted * shifted, -1, keepdims=True) + EPSILON)
        hat = shifted * inverse
        gain = r.conv_gain[...]
        normed = hat * gain
        logistic = jax.nn.sigmoid(normed)
        r.low[at, :] = (normed * logistic).astype(BF16)
        scaled = r.act_grad[at, :] * (logistic * (1.0 + normed * (1.0 - logistic))) * gain
        grad = inverse * (
            scaled - jnp.mean(scaled, -1, keepdims=True) - hat * jnp.mean(scaled * hat, -1, keepdims=True)
        )
        r.conv_grad[at, :] = grad.astype(BF16)
        for c in range(pairs):
            r.g_pad[c, pl.ds(i * SUB + SUB, SUB), :] = grad[:, c * LANES : (c + 1) * LANES]

    rows_loop(frames // SUB, mid_rows)
    edge_out = edges(r.conv_grad, r.halo_out, 2)
    for copy in edge_out:
        copy.start()

    out_sum.give_left(r.low)
    outward(0)

    for copy in edge_out:
        copy.wait()
    land(r.halo_out, r.g_pad)

    def back_tile(c):
        at = span(c, LANES)
        own = r.x_pad[c, pl.ds(SUB, frames), :]
        total = jnp.zeros((frames, LANES), F32)
        for tap in range(taps):
            moved = r.g_pad[c, pl.ds(SUB - reach + tap, frames), :] * r.same[tap]
            back = taps - 1 - tap
            total = total + r.taps_f[back : back + 1, at] * moved
            r.tap_sum[back : back + 1, at] = jnp.sum(own * moved, 0, keepdims=True)
        linear, logistic = r.linear[:, at], r.logistic[:, at]
        gated = total * logistic
        r.both_grad[:, at] = gated.astype(BF16)
        r.both_grad[:, span(c + pairs, LANES)] = (gated * linear * (1.0 - logistic)).astype(BF16)

    tap_rows = r.tap_sum.shape[0]
    r.tap_sum[pl.ds(tap_rows - SUB, SUB), :] = jnp.zeros((SUB, width), F32)
    loop(pairs, back_tile)

    everyone = bits_of(n, q)

    def tap_copy(k):
        return remote(
            r.tap_out.at[k], r.tap_in.at[k], r.tap_send.at[k], r.tap_recv.at[k], **partner(everyone[k])
        )

    def tap_start(k):
        rounded = r.tap_sum[...].astype(BF16)
        r.tap_out[k] = rounded
        tap_copy(k).start()

    def tap_finish(k):
        tap_copy(k).wait()
        r.tap_sum[...] = r.tap_out[k].astype(F32) + r.tap_in[k].astype(F32)

    tap_at = [0]

    def tap_next():
        if tap_at[0] < len(everyone):
            tap_finish(tap_at[0])
            tap_at[0] += 1
            if tap_at[0] < len(everyone):
                tap_start(tap_at[0])

    tap_start(0)
    outward(1)
    out_sum.multiply()

    def back_in_tile(i):
        r.work[:, span(i, TILE)] = dot_t(r.both_grad[...], r.pin[span(i, TILE), :])

    tap_next()
    loop(tiles, back_in_tile)

    def stream_rows(i):
        at = span(i, SUB)
        hat = r.hat_in[at, :]
        scaled = r.work[at, :] * r.norm_gain[...]
        grad = r.inv_in[at, :][:, :1] * (
            scaled - jnp.mean(scaled, -1, keepdims=True) - hat * jnp.mean(scaled * hat, -1, keepdims=True)
        )
        done = (r.g_in[at, :].astype(F32) + grad).astype(BF16)
        r.in_right[at, :] = done
        for h in range(2):
            r.stream_two[h, at, :] = done[:, h * half_cols : (h + 1) * half_cols]

    rows_loop(frames // SUB, stream_rows)
    twos = [r.stream_two.at[h] for h in range(2)]
    inters_s = [r.inter_a, r.inter_b]
    stages_s = [r.stage_s.at[h] for h in range(2)]
    slots_s = [r.slot_s.at[h] for h in range(2)]
    wide_s = [widen(slots_s[h], r.wide_send_s, r.wide_recv_s, (q - 1) * h) for h in range(2)]
    for h in range(2):
        spread(twos[h], inters_s[h], 6 + h)
    for h in range(2):
        spread_own(twos[h], inters_s[h])
    in_sum.give_right()
    tap_next()
    out_sum.step()
    in_sum.multiply()

    def pass_on(h):
        settle(inters_s[h], 6 + h)
        deliver(inters_s[h], stages_s[h], slots_s[h], 8 + h)

    def pass_wide(h):
        settle(stages_s[h], 8 + h)
        start(wide_s[h])

    def slot_weights(i, b):
        rows, at = span(b, frames), span(i, LANES)
        queries = stacked(r.slot[0, rows, at], scale)
        return softmax(dot_t(queries, r.slot[1, :, at]), r.slot_bias[rows, :])

    def weigh(first_pair, count):
        if r.kept.shape[0] < pairs:
            return

        def one(i):
            def of_block(b):
                r.kept[first_pair + i, b] = slot_weights(first_pair + i, b)

            loop(q, of_block)

        loop(count, one)

    pass_on(0)
    outward(2)
    tap_next()
    pass_on(1)
    wait(wide[0])
    wait(wide[1])
    weigh(0, pairs // 2)
    in_sum.step()
    pass_wide(0)
    out_sum.step()
    tap_next()
    weigh(pairs // 2, pairs - pairs // 2)
    pass_wide(1)
    tap_next()
    in_sum.step()
    out_sum.step()
    wait(wide[2])
    wait(wide_s[0])
    wait(wide_s[1])
    for h in range(2):
        r.stream_grad[0, :, pl.ds(h * half_cols, half_cols)] = r.slot_s[h, pl.ds(0, frames), :]

    def mixed_tile(i):
        r.mixed_grad[:, span(i, TILE)] = (
            dot_t(r.slot_s[0], r.ao[span(i, TILE), pl.ds(0, half_cols)])
            + dot_t(r.slot_s[1], r.ao[span(i, TILE), pl.ds(half_cols, half_cols)])
        ).astype(BF16)

    loop(tiles, mixed_tile)

    def back_pair(i):
        at = span(i, LANES)
        key_two, value_two = r.slot[1, :, at], r.slot[2, :, at]

        def block(b):
            rows = span(b, frames)
            queries = stacked(r.slot[0, rows, at], scale)
            grads = stacked(r.mixed_grad[rows, at])
            weights = r.kept[i, b] if r.kept.shape[0] == pairs else slot_weights(i, b)
            slope = dot_t(grads, value_two)
            delta = jnp.sum(weights * slope, -1, keepdims=True)
            score_grad = (weights * (slope - delta)).astype(BF16)
            return (
                score_grad,
                t_dot(score_grad[:, :frames], queries),
                t_dot(weights[:, :frames].astype(BF16), grads),
            )

        score_grad, key_part, value_part = block(0)
        r.query_grad[0, :, at] = (merged(dot(score_grad, key_two)) * scale).astype(BF16)

        def more(b, carry):
            _, key_more, value_more = block(b)
            return carry[0] + key_more, carry[1] + value_more

        key_part, value_part = lax.fori_loop(1, q, more, (key_part, value_part))
        r.key_grad[0, :, at] = key_part.astype(BF16)
        r.value_grad[0, :, at] = value_part.astype(BF16)

    def between(first_pair, count):
        loop(count, lambda i: back_pair(first_pair + i))

    rest = max(in_sum.depth - in_sum.k, 1)
    done = 0
    for k in range(rest):
        until = pairs * (k + 1) // rest
        between(done, until - done)
        done = until
        out_sum.step()
        in_sum.step()
    while tap_at[0] < len(everyone):
        tap_next()
    while max(in_sum.depth - in_sum.k, out_sum.depth - out_sum.k) > 0:
        out_sum.step()
        in_sum.step()
    r.kernel_grad[...] = r.tap_sum[pl.ds(0, taps), :]
    r.proj[:, pl.ds(0, width)] = r.in_total[pl.ds(0, gran), :]
    r.proj[:, pl.ds(width, width)] = r.out_total[pl.ds(0, gran), :]


def handed_out(*refs):
    count = len(refs) // 2
    for i in range(count):
        refs[count + i][...] = refs[i][...]


def swapped(cells, axis, bit):
    return lax.ppermute(cells, axis, [(i, i ^ (1 << bit)) for i in range(lax.axis_size(axis))])


def finished(cells, left, low):
    for axis, bit, place in sorted(left, key=lambda e: -e[2]):
        mine = (lax.axis_index(axis) >> bit) & 1
        split = cells.reshape(2, -1, cells.shape[1])
        out = lax.dynamic_index_in_dim(split, 1 - mine, 0, keepdims=False)
        cells = lax.dynamic_index_in_dim(split, mine, 0, keepdims=False) + swapped(
            out.astype(BF16), axis, bit
        ).astype(F32)
    return cells


def per_device(
    queries, keys, values, stream, cotangent, attn_out, point_in, kernel, point_out, norm_gain, conv_gain, segments, plan
):
    n, q = lax.axis_size("dp"), lax.axis_size("seq")
    frames, width = queries.shape[1:]
    taps = kernel.shape[0]
    whole = q * frames
    pairs = width // LANES
    rows_c, cols_c = chunking(n, frames, width)
    rows_s, cols_s = chunking(n, frames, width // 2)
    keep = pairs * q * 2 * frames * whole * 4 <= KEPT
    order, left, low = split_bits(n, q, width)
    depth = len(order)
    everyone = len(bits_of(n, q))
    parts = width // TILE
    tap_rows = -(-taps // SUB) * SUB
    any_, vmem, smem = (pl.BlockSpec(memory_space=m) for m in (pl.ANY, pltpu.VMEM, pltpu.SMEM))
    ins = dict(
        queries=any_,
        keys=any_,
        values=any_,
        stream=any_,
        cotangent=any_,
        attn_out=any_,
        point_in=any_,
        kernel=vmem,
        point_out=any_,
        norm_gain=vmem,
        conv_gain=vmem,
        segments=vmem,
        plan=smem,
    )
    low_block = jax.ShapeDtypeStruct((1, frames, width), BF16)
    outs = dict(
        query_grad=low_block,
        key_grad=low_block,
        value_grad=low_block,
        stream_grad=low_block,
        kernel_grad=jax.ShapeDtypeStruct((taps, width), F32),
        proj=jax.ShapeDtypeStruct((width >> depth, 2 * width), F32),
    )
    dma = pltpu.SemaphoreType.DMA

    def low_(*shape):
        return pltpu.VMEM(shape, BF16)

    def full_(*shape):
        return pltpu.VMEM(shape, F32)

    padded = frames + 2 * SUB
    sums = {}
    for name, group, sequences in zip(("in_", "out_"), groups_of(order), (2, 1)):
        members, rows = 1 << len(group), width >> len(group)
        made = dict(
            left=low_(rows, members * frames),
            right=low_(members * frames, width),
            staged=low_(members - 1, rows, frames),
            total=full_(rows, width),
            out=low_(rows, width),
            swap=dma((2, 2 * members)),
            sum=dma((2, sequences * (depth - len(group)))),
        )
        made.update({"in": low_(rows, width)})
        sums.update({name + key: value for key, value in made.items()})
    scratch = dict(
        g_in=low_(frames, width),
        po=low_(width, width),
        q_in=low_(frames, width),
        x_in=low_(frames, width),
        ao=low_(width, width),
        pin=low_(width, 2 * width),
        k_all=low_(whole, width),
        v_all=low_(whole, width),
        inter_q=low_(n, rows_c, cols_c),
        inter_k=low_(n, rows_c, cols_c),
        inter_v=low_(n, rows_c, cols_c),
        stage=low_(3, n, rows_c, cols_c),
        slot=low_(3, whole, width),
        inter_a=low_(n, rows_s, cols_s),
        inter_b=low_(n, rows_s, cols_s),
        stage_s=low_(2, n, rows_s, cols_s),
        slot_s=low_(2, whole, width // 2),
        kept=full_(pairs if keep else 1, q, 2 * frames, whole),
        bias=full_(frames, whole),
        slot_bias=full_(whole, whole),
        id_pad=full_(padded, LANES),
        same=full_(taps, frames, LANES),
        taps_f=full_(tap_rows, width),
        act_grad=full_(frames, width),
        mixed=low_(frames, width),
        hat_in=full_(frames, width),
        inv_in=full_(frames, LANES),
        low=low_(frames, width),
        linear=full_(frames, width),
        logistic=full_(frames, width),
        conv_in=low_(frames, width),
        conv_grad=low_(frames, width),
        x_pad=full_(pairs, padded, LANES),
        g_pad=full_(pairs, padded, LANES),
        halo_in=low_(2, SUB, width),
        halo_out=low_(2, SUB, width),
        work=full_(frames, width),
        turned=low_(width, frames),
        **sums,
        tap_sum=full_(tap_rows, width),
        tap_out=low_(everyone, tap_rows, width),
        tap_in=low_(everyone, tap_rows, width),
        both_grad=low_(frames, 2 * width),
        stream_two=low_(2, frames, width // 2),
        mixed_grad=low_(whole, width),
        load_sem=dma((8,)),
        kv_send=dma(((q - 1) * parts * 2,)),
        kv_recv=dma(((q - 1) * parts * 2,)),
        route_sem=dma((20,)),
        wide_send=dma(((q - 1) * 3,)),
        wide_recv=dma(((q - 1) * 3,)),
        wide_send_s=dma((2 * (q - 1),)),
        wide_recv_s=dma((2 * (q - 1),)),
        edge_send=dma((4,)),
        edge_recv=dma((4,)),
        tap_send=dma((everyone,)),
        tap_recv=dma((everyone,)),
    )
    names = (*ins, *outs, *scratch)
    query_grad, key_grad, value_grad, stream_grad, kernel_grad, proj = pl.pallas_call(
        functools.partial(body, n, q, names),
        out_shape=tuple(outs.values()),
        in_specs=list(ins.values()),
        out_specs=(vmem,) * len(outs),
        scratch_shapes=list(scratch.values()),
        compiler_params=pltpu.CompilerParams(
            collective_id=0, has_side_effects=True, vmem_limit_bytes=60 * 2**20
        ),
    )(
        queries,
        keys,
        values,
        stream,
        cotangent,
        attn_out,
        point_in,
        kernel,
        point_out,
        norm_gain.reshape(1, width),
        conv_gain.reshape(1, width),
        segments,
        plan,
    )
    results = (query_grad, key_grad, value_grad, stream_grad, kernel_grad, finished(proj, left, low))
    return pl.pallas_call(
        handed_out,
        out_shape=tuple(jax.ShapeDtypeStruct(x.shape, x.dtype) for x in results),
        in_specs=[vmem] * len(results),
        out_specs=(vmem,) * len(results),
    )(*results)


def solution(mesh):
    rows = P("dp", "seq", None)
    return jax.shard_map(
        per_device,
        mesh=mesh,
        in_specs=(rows,) * 5 + (P(),) * 8,
        out_specs=(rows,) * 4 + (P(), P(("dp", "seq"), None)),
        check_vma=False,
    )
```
